32 devices in a mesh: elem: 8 (over z, x), inner: 4 (over y, core).
Axes of the slice: x: 2, y: 2, z: 4, core: 2. Of those that a mesh axis runs over, the one named last changes fastest.
Arguments:
- basis: bfloat16 [16, 4, 512, 4096], P('elem', None, 'inner'), may hold values from -6 to 6, as said below
- potential: float32 [16, 4096], P('elem'), may hold values from 0.2 to 2
- face_index: int32 [16, 2, 128], P('elem'), may hold values from 0 to 4095, as said below
- face_match: int32 [16, 128], P('elem'), may hold values from 0 to 127, each once within a row
- vectors: bfloat16 [16, 512, 1024], P('elem', None, 'inner'), may hold values from -6 to 6
Outputs:
- filtered: float32 [16, 512, 1024], P('elem', None, 'inner')
The draws below stay inside these ranges and needn't reach their ends.
Inputs may be any that keep to these rules, and one draw needn't show every extreme that they name: `basis`: entries are independent, of mean zero and variance one. `face_index`: within one element the 256 listed grid points are distinct. Row e is a permutation; right-face point f of element e - 1 (modulo 16) meets left-face point face_match[e, f] of element e.
All inputs are finite; a program needn't handle non-finite values.
Results may differ from the reference program's by a relative error of at most 0.007.
The reference program's roundings to bfloat16 on the way count: a program that leaves them out, or rounds other values in their place, can miss the bound.
Values may be sent and summed in bfloat16 or wider, within the bound.
A program may use at most 64 MiB of HBM per device.

```python
import math
import jax
import jax.numpy as jnp
from jax import lax

NB = 512
NG = 4096
F = 128
STEPS = 6
NE = 16
NV = 1024


def draw_basis(key, part):
    shape = (NE, 4, NB, NG)
    values = jnp.clip(jax.random.normal(key, shape, jnp.float32), -6.0, 6.0)
    return values.astype(jnp.bfloat16)


def draw_face_index(key, part):
    element_keys = jax.random.split(jax.random.fold_in(key, 7), NE)
    shuffled = jax.vmap(lambda subkey: jax.random.permutation(subkey, NG))(element_keys).astype(jnp.int32)
    leading_row = shuffled[0]
    moved = leading_row[0]
    leading_row = jnp.where(leading_row == 0, moved, leading_row).at[0].set(0)
    moved = leading_row[1]
    leading_row = jnp.where(leading_row == NG - 1, moved, leading_row).at[1].set(NG - 1)
    shuffled = shuffled.at[0].set(leading_row)
    return shuffled[:, :2 * F].reshape(NE, 2, F).astype(jnp.int32)


def level_of(rng, extent, cuts, least, largest):
    level, own = 1.0, jax.random.fold_in(rng, 6)
    for dim, shards_of in cuts:
        heights = jnp.exp(jax.random.uniform(jax.random.fold_in(own, dim), (shards_of,), jnp.float32, least / len(cuts), largest / len(cuts)))
        level = level * jnp.repeat(heights, extent[dim] // shards_of).reshape([-1 if axis == dim else 1 for axis in range(len(extent))])
    return level


def gaussian(own_key, dims, deviation, bound, cuts=(), held_as=jnp.bfloat16):
    level = level_of(own_key, dims, cuts, -0.22, 0.18) if cuts else 1.0
    entries = jax.random.normal(own_key, dims, jnp.float32) * deviation * level
    return jnp.minimum(jnp.maximum(entries, -bound), bound).astype(held_as)


def setup_inputs(seed: int = 0) -> dict:
    seeds = jax.random.split(jax.random.key(seed), 6)
    basis = draw_basis(jax.random.fold_in(seeds[5], 71), 0)
    potential = jnp.clip(jnp.exp(math.log(2.0) - 2.3025851 * jax.random.uniform(seeds[1], (NE, NG), jnp.float32) ** level_of(seeds[1], (NE, NG), ((0, 8),), -0.2, 0.2)), 0.2, 2.0)
    face_index = draw_face_index(jax.random.fold_in(seeds[5], 71), 0)
    face_match = jax.vmap(lambda own: jax.random.permutation(own, F))(jax.random.split(seeds[3], NE)).reshape((NE, F)).astype(jnp.int32)
    vectors = gaussian(seeds[4], (NE, NB, NV), 1.0, 6.0, ((0, 8), (2, 4)))
    return dict(basis=basis, potential=potential, face_index=face_index, face_match=face_match, vectors=vectors)


CENTER = 5.25
HALF_WIDTH = 2.75

def chebyshev_norm(count):
    ratio = (CENTER - 1.0) / HALF_WIDTH
    root = ratio + (ratio * ratio - 1.0) ** 0.5
    return 0.5 * (root ** count + root ** (-count))

def face_pair(leading, second):
    return jnp.einsum('nsaf,nsbf->nab', leading.astype(jnp.float32), jnp.flip(second, 1).astype(jnp.float32)) / (4.0 * F)

def element_terms(inputs):
    element_block, element_potential, right_points, left_points = inputs
    scaled = (jnp.sqrt(element_potential)[None, :] * element_block[0].astype(jnp.float32)).astype(jnp.bfloat16)
    volume = jnp.dot(scaled, scaled.T, preferred_element_type=jnp.float32)
    slopes = element_block[1:4].astype(jnp.float32)
    kinetic = jnp.einsum('cag,cbg->ab', slopes, slopes)
    gram_sum = (volume + 0.5 * kinetic) / NG
    right_found = jnp.take(element_block[0:2], right_points, axis=2)
    left_found = jnp.take(element_block[0:2], left_points, axis=2)
    right_flux = (0.5 * right_found[0].astype(jnp.float32) - 0.25 * right_found[1].astype(jnp.float32)).astype(jnp.bfloat16)
    left_flux = (-0.5 * left_found[0].astype(jnp.float32) - 0.25 * left_found[1].astype(jnp.float32)).astype(jnp.bfloat16)
    right_sides = jnp.stack((right_flux, right_found[0]))
    left_sides = jnp.stack((left_flux, -left_found[0]))
    return (gram_sum, right_sides, left_sides)

def reference(basis, potential, face_index, face_match, vectors):
    left_points = jnp.take_along_axis(face_index[:, 0, :], face_match, axis=1)
    gram_sum, right_sides, left_sides = lax.map(element_terms, (basis, potential, face_index[:, 1, :], left_points))
    diagonal = (gram_sum + face_pair(right_sides, right_sides) + face_pair(left_sides, left_sides)).astype(jnp.bfloat16)
    upper_blocks = face_pair(right_sides, jnp.roll(left_sides, -1, axis=0)).astype(jnp.bfloat16)
    diagonal_wide = diagonal.astype(jnp.float32)
    upper_wide = upper_blocks.astype(jnp.float32)
    lower_wide = jnp.roll(upper_wide, 1, axis=0)

    def apply_operator(current_bf):
        wide = current_bf.astype(jnp.float32)
        result = jnp.einsum('eab,ebv->eav', diagonal_wide, wide)
        result = result + jnp.einsum('eab,ebv->eav', upper_wide, jnp.roll(wide, -1, axis=0))
        result = result + jnp.einsum('eba,ebv->eav', lower_wide, jnp.roll(wide, 1, axis=0))
        return result
    previous = vectors.astype(jnp.float32)
    current = (apply_operator(vectors) - CENTER * previous) / HALF_WIDTH
    for iteration in range(1, STEPS):
        applied = apply_operator(current.astype(jnp.bfloat16))
        following = 2.0 * (applied - CENTER * current) / HALF_WIDTH - previous
        previous = current
        current = following
    return current / chebyshev_norm(STEPS)
```

```python
import functools

import jax
import jax.numpy as jnp
from jax import lax
from jax.experimental import pallas as pl
from jax.experimental.pallas import tpu as pltpu
from jax.sharding import PartitionSpec as P

MESH = pl.DeviceIdType.MESH

NG = 4096
F = 128
STEPS = 6


CENTER = 5.25
HALF_WIDTH = 2.75


def padded_2(cells, sides, width):
    for axis, dim in sides:
        count = lax.axis_size(axis)
        head = lax.slice_in_dim(cells, 0, width, axis=dim)
        tail = lax.slice_in_dim(cells, cells.shape[dim] - width, cells.shape[dim], axis=dim)
        cells = jnp.concatenate(
            [
                lax.ppermute(tail, axis, [(i, (i + 1) % count) for i in range(count)]),
                cells,
                lax.ppermute(head, axis, [((i + 1) % count, i) for i in range(count)]),
            ],
            axis=dim,
        )
    return cells


def chebyshev_norm(count):
    ratio = (CENTER - 1.0) / HALF_WIDTH
    root = ratio + (ratio * ratio - 1.0) ** 0.5
    return 0.5 * (root**count + root ** (-count))


def face_pair(leading, second):
    return jnp.einsum(
        "nsaf,nsbf->nab", leading, jnp.flip(second, 1), preferred_element_type=jnp.float32
    ) / (4.0 * F)


def gram_terms(exchanged):
    scaled = exchanged[:, 0]
    slopes = exchanged[:, 1:4]
    volume = jnp.einsum("nag,nbg->nab", scaled, scaled, preferred_element_type=jnp.float32)
    kinetic = jnp.einsum("ncag,ncbg->nab", slopes, slopes, preferred_element_type=jnp.float32)
    return (volume + 0.5 * kinetic) / NG


def face_values(element_block, element_points):
    return jnp.take(element_block[0:2], element_points, axis=2)


def per_device(basis, potential, face_index, face_match, vectors):
    elements = basis.shape[0]
    scaled = (jnp.sqrt(potential)[:, None, :] * basis[:, 0].astype(jnp.float32)).astype(
        jnp.bfloat16
    )
    grid_pack = jnp.concatenate((scaled[:, None], basis[:, 1:4]), axis=1)
    gram_part = gram_terms(
        lax.all_to_all(grid_pack, "inner", split_axis=3, concat_axis=2, tiled=True)
    )
    left_points = jnp.take_along_axis(face_index[:, 0, :], face_match, axis=1)
    right_found = jax.vmap(face_values)(basis, face_index[:, 1, :])
    left_found = jax.vmap(face_values)(basis, left_points)
    right_flux = (
        0.5 * right_found[:, 0].astype(jnp.float32) - 0.25 * right_found[:, 1].astype(jnp.float32)
    ).astype(jnp.bfloat16)
    left_flux = (
        -0.5 * left_found[:, 0].astype(jnp.float32) - 0.25 * left_found[:, 1].astype(jnp.float32)
    ).astype(jnp.bfloat16)
    right_sides = jnp.stack((right_flux, right_found[:, 0]), axis=1)
    left_sides = jnp.stack((left_flux, -left_found[:, 0]), axis=1)
    rim_sides = jnp.stack((left_sides[0], right_sides[-1]))
    rim_padded = padded_2(rim_sides, (("elem", 0),), 1)
    from_left = rim_padded[0:1]
    from_right = rim_padded[3:4]
    local_sides = jnp.concatenate((right_sides, left_sides, from_left, from_right), axis=0)
    full_sides = lax.all_gather(local_sides, "inner", axis=2, tiled=True)
    full_rights = full_sides[:elements]
    full_lefts = full_sides[elements : 2 * elements]
    full_next = full_sides[2 * elements + 1 : 2 * elements + 2]
    full_prev = full_sides[2 * elements : 2 * elements + 1]
    next_lefts = jnp.concatenate((full_lefts[1:], full_next), axis=0)
    gram_sum = lax.psum(gram_part, "inner")
    diagonal = (
        gram_sum + face_pair(full_rights, full_rights) + face_pair(full_lefts, full_lefts)
    ).astype(jnp.bfloat16)
    upper_blocks = face_pair(full_rights, next_lefts).astype(jnp.bfloat16)
    first_lower = face_pair(full_prev, full_lefts[0:1]).astype(jnp.bfloat16)
    lower_blocks = jnp.concatenate((first_lower, upper_blocks[:-1]), axis=0)

    def apply_operator(current_bf):
        padded = padded_2(current_bf, (("elem", 0),), 1)
        result = jnp.einsum(
            "jab,jbv->jav", diagonal, current_bf, preferred_element_type=jnp.float32
        )
        result = result + jnp.einsum(
            "jab,jbv->jav", upper_blocks, padded[2:], preferred_element_type=jnp.float32
        )
        result = result + jnp.einsum(
            "jba,jbv->jav", lower_blocks, padded[:-2], preferred_element_type=jnp.float32
        )
        return result

    previous = vectors.astype(jnp.float32)
    current = (apply_operator(vectors) - CENTER * previous) / HALF_WIDTH
    for iteration in range(1, STEPS):
        applied = apply_operator(current.astype(jnp.bfloat16))
        following = 2.0 * (applied - CENTER * current) / HALF_WIDTH - previous
        previous = current
        current = following
    return current / chebyshev_norm(STEPS)


def assemble_and_filter(
    inner,
    ring,
    basis,
    potential,
    face_index,
    face_match,
    vectors,
    out,
    own,
    cross,
    nodal,
    faces,
    turned,
    operator,
    own_sum,
    cross_sum,
    own_other,
    cross_other,
    state,
    links,
    edges,
    current,
    previous,
    local_sem,
    pair_send,
    pair_recv,
    cross_send,
    cross_recv,
    face_send,
    face_recv,
    sum_send,
    sum_recv,
    block_send,
    block_recv,
    halo_send,
    halo_recv,
):
    elements, parts, rows, grid = basis.shape
    total = rows * inner
    faced = face_index.shape[2]
    half = grid // 2
    step_k = min(half, 512)
    columns = vectors.shape[2] // 2
    me = lax.axis_index("inner")
    place = lax.axis_index("elem")
    chip, core = me // 2, lax.rem(me, 2)
    partner = chip * 2 + (1 - core)
    far = 1 - chip
    following = lax.rem(place + 1, ring)
    preceding = lax.rem(place + ring - 1, ring)
    peers = [lax.rem(me + d, inner) for d in range(1, inner)]
    across = far * 2 + core
    diagonal_peer = far * 2 + (1 - core)
    routes = ((0, partner), (1, across))
    sources = (partner, across, diagonal_peer)

    def aligned(index, size):
        return pl.ds(pl.multiple_of(index * size, size), size)

    def send(src, dst, send_sem, recv_sem, **where):
        return pltpu.make_async_remote_copy(
            src_ref=src,
            dst_ref=dst,
            send_sem=send_sem,
            recv_sem=recv_sem,
            device_id=where,
            device_id_type=MESH,
        )

    barrier = pltpu.get_barrier_semaphore()
    for peer in peers:
        pl.semaphore_signal(barrier, inc=1, device_id={"inner": peer}, device_id_type=MESH)
    for peer in (preceding, following):
        pl.semaphore_signal(barrier, inc=1, device_id={"elem": peer}, device_id_type=MESH)

    nodal_copy = pltpu.make_async_copy(basis.at[:, 0:2], nodal, local_sem.at[0, 0])
    nodal_copy.start()
    local = {}
    for e in range(elements):
        for k in range(parts):
            local[e, k] = pltpu.make_async_copy(
                basis.at[e, k, :, aligned(core, half)],
                own.at[e, k, aligned(core, rows)],
                local_sem.at[1 + e, k],
            )
            local[e, k].start()

    pl.semaphore_wait(barrier, inner + 1)

    sends = []

    def launch(copy):
        copy.start()
        sends.append(copy)

    def start_cross(k):
        for other in range(2):
            side = lax.rem(core + other, 2)
            launch(
                send(
                    basis.at[far, k, :, aligned(side, half)],
                    cross.at[k, aligned(core, rows)],
                    cross_send.at[other, k],
                    cross_recv.at[other, k],
                    inner=far * 2 + side,
                )
            )

    start_cross(0)
    for e in range(elements):
        for k in range(parts):
            launch(
                send(
                    basis.at[e, k, :, aligned(1 - core, half)],
                    own.at[e, k, aligned(core, rows)],
                    pair_send.at[e, k],
                    pair_recv.at[e, k],
                    inner=partner,
                )
            )

    low, high = pl.ds(0, 2 * faced), pl.ds(2 * faced, 2 * faced)

    def halo(k, h, side):
        return send(
            edges.at[k, h, side],
            links.at[k, h, 0, high] if side else links.at[k, h, elements - 1, low],
            halo_send.at[k, h, side],
            halo_recv.at[k, h, side],
            elem=following if side else preceding,
        )

    nodal_copy.wait()
    square = (faced, faced)
    for e in range(elements):
        down = lax.broadcasted_iota(jnp.int32, square, 0)
        along = lax.broadcasted_iota(jnp.int32, square, 1)
        left_row = jnp.broadcast_to(face_index[e, 0:1, :], square)
        left_column = jnp.sum(jnp.where(down == along, left_row, 0), axis=1, keepdims=True)
        matched = jnp.broadcast_to(face_match[e : e + 1, :], square) == down
        left_points = jnp.sum(
            jnp.where(matched, jnp.broadcast_to(left_column, square), 0), axis=0, keepdims=True
        )
        points = jnp.concatenate([face_index[e, 1:2, :], left_points], axis=1)

        def pick(index, found, e=e, points=points):
            offset = pl.multiple_of(index * step_k, step_k)
            spots = lax.broadcasted_iota(jnp.int32, (step_k, 2 * faced), 0) + offset
            chosen = (spots == jnp.broadcast_to(points, spots.shape)).astype(jnp.float32)
            chosen = chosen.astype(jnp.bfloat16)
            return tuple(
                found[k]
                + jnp.dot(
                    nodal[e, k, :, pl.ds(offset, step_k)],
                    chosen,
                    preferred_element_type=jnp.float32,
                )
                for k in range(2)
            )

        start = jnp.zeros((rows, 2 * faced), jnp.float32)
        value, slope = lax.fori_loop(0, grid // step_k, pick, (start, start))
        right_value, left_value = value[:, :faced], value[:, faced:]
        right_slope, left_slope = slope[:, :faced], slope[:, faced:]
        mine = aligned(me, rows)
        pieces = (
            0.5 * right_value - 0.25 * right_slope,
            right_value,
            -0.5 * left_value - 0.25 * left_slope,
            -left_value,
        )
        for index, piece in enumerate(pieces):
            faces[e, mine, index * faced : (index + 1) * faced] = piece.astype(jnp.bfloat16)
    def face_copy(d, e, owner, target):
        block = faces.at[e, aligned(owner, rows)]
        return send(block, block, face_send.at[d, e], face_recv.at[d, e], inner=target)

    for d, peer in routes:
        for e in range(elements):
            launch(face_copy(d, e, me, peer))
    for k in range(1, parts - 1):
        start_cross(k)

    def product(left, right):
        return lax.dot_general(
            left, right, (((1,), (1,)), ((), ())), preferred_element_type=jnp.float32
        )

    def swapped(side):
        cut = [side[:, k * faced : (k + 1) * faced] for k in range(side.shape[1] // faced)]
        order = [k + 1 - 2 * (k % 2) for k in range(len(cut))]
        return jnp.concatenate([cut[k] for k in order], axis=1)

    def weighted(row_left, row_right, left, right, k, target, scale_left):
        @pl.loop(0, half // step_k)
        def _(index):
            offset = pl.multiple_of(index * step_k, step_k)
            span = pl.ds(offset, step_k)
            there = pl.ds(pl.multiple_of(core * half + offset, step_k), step_k)
            one = left[:, span]
            if k == 0 and scale_left:
                root = jnp.sqrt(potential[row_left, there])
                one = (one.astype(jnp.float32) * root).astype(jnp.bfloat16)
                left[:, span] = one
            two = one if right is left else right[:, span]
            if k == 0 and right is not left:
                root = jnp.sqrt(potential[row_right, there])
                two = (two.astype(jnp.float32) * root).astype(jnp.bfloat16)
            term = product(one, two)
            target[...] += term if k == 0 else 0.5 * term

    for e in range(elements):
        own_sum[e] = jnp.zeros(own_sum.shape[1:], jnp.float32)
        for k in range(parts):
            local[e, k].wait()
            send(
                basis.at[e, k, :, aligned(core, half)],
                own.at[e, k, aligned(1 - core, rows)],
                pair_send.at[e, k],
                pair_recv.at[e, k],
                inner=partner,
            ).wait_recv()
            block = own.at[e, k]
            weighted(pl.ds(e, 1), pl.ds(e, 1), block, block, k, own_sum.at[e], True)
        launch(
            send(
                own_sum.at[e, aligned(1 - core, rows)],
                own_other.at[e],
                sum_send.at[e],
                sum_recv.at[e],
                inner=partner,
            )
        )

    for e in range(elements):
        face_copy(1, e, across, across).wait_recv()
        launch(face_copy(2, e, across, partner))
    for e in range(elements):
        face_copy(0, e, partner, partner).wait_recv()
        face_copy(2, e, diagonal_peer, partner).wait_recv()
    for e in range(elements):
        for index in range(4):
            cut = faces[e, :, index * faced : (index + 1) * faced]
            turn = index + 1 - 2 * (index % 2)
            turned[e, turn * faced : (turn + 1) * faced, :] = cut.T

    def coupled(e, cut, values):
        found = jnp.dot(turned[e, cut, :], values, preferred_element_type=jnp.float32)
        return (found * (1.0 / (4.0 * faced))).astype(jnp.bfloat16)

    def edge(k, h, side, values):
        edges[k, h, side] = coupled((elements - 1) * side, low if side else high, values)
        launch(halo(k, h, side))

    def inside(k, h, of):
        for e in range(elements - 1):
            links[k, h, e, low] = coupled(e + 1, high, of(e + 1))
            links[k, h, e + 1, high] = coupled(e, low, of(e))

    def given(h):
        return lambda e: vectors[e, :, h * columns : (h + 1) * columns]

    for h in range(2):
        for side in range(2):
            edge(0, h, side, given(h)((elements - 1) * side))
    for h in range(2):
        inside(0, h, given(h))

    def diagonal(e, to_chip):
        return product(
            faces[e, aligned(me, rows)], swapped(faces[e, aligned(to_chip, 2 * rows)])
        ) / (4.0 * faced)

    def block_of(e, owner, to_chip):
        return operator.at[e, aligned(owner, rows), aligned(to_chip, 2 * rows)]

    def block_copy(d, slot, owner, target):
        owner_chip = owner // 2
        e = slot if slot < elements else owner_chip
        block = block_of(e, owner, owner_chip if slot < elements else 1 - owner_chip)
        return send(
            block, block, block_send.at[d, slot], block_recv.at[d, slot], inner=target
        )

    for e in range(elements):
        send(
            own_sum.at[e, aligned(core, rows)],
            own_other.at[e],
            sum_send.at[e],
            sum_recv.at[e],
            inner=partner,
        ).wait_recv()
        gram = (own_sum[e, aligned(core, rows)] + own_other[e]) / grid
        block_of(e, me, chip)[...] = (gram + diagonal(e, chip)).astype(jnp.bfloat16)
        for d, peer in routes:
            launch(block_copy(d, e, me, peer))
    start_cross(parts - 1)

    for h in range(2):
        for e in range(elements):
            piece = vectors[e, :, h * columns : (h + 1) * columns]
            current[h, e] = piece.astype(jnp.float32)

    norm = chebyshev_norm(STEPS)
    tile = min(total, 256)
    wide = 2 * rows

    def applied_by(e, some, begin, length, values):
        return jnp.dot(
            operator[e, some, begin : begin + length],
            values,
            preferred_element_type=jnp.float32,
        )

    def through(k, h, e, some, cut):
        return jnp.dot(
            faces[e, some, cut], links[k, h, e, cut], preferred_element_type=jnp.float32
        )

    def update(k, h, e, some, applied):
        scale = (2.0 if k else 1.0) / HALF_WIDTH
        now = current[h, e, some]
        moved = scale * applied - (scale * CENTER) * now
        if k:
            moved = moved - previous[h, e, some]
        if k + 1 == STEPS:
            out[e, some, h * columns : (h + 1) * columns] = moved * (1.0 / norm)
        else:
            previous[h, e, some] = now
            current[h, e, some] = moved
            state[h, e, some] = moved.astype(jnp.bfloat16)

    def before(k, h):
        @pl.loop(0, total // tile)
        def _(index):
            some = pl.ds(pl.multiple_of(index * tile, tile), tile)
            for e in range(elements):
                found = applied_by(e, some, 0, total, state[h, e])
                if e:
                    found += through(k, h, e, some, high)
                if e + 1 < elements:
                    found += through(k, h, e, some, low)
                out[e, some, h * columns : (h + 1) * columns] = found

    def after(k, h, side):
        e = (elements - 1) * (1 - side)
        halo(k, h, side).wait_recv()

        @pl.loop(0, total // tile)
        def _(index):
            some = pl.ds(pl.multiple_of(index * tile, tile), tile)
            applied = out[e, some, h * columns : (h + 1) * columns]
            applied += through(k, h, e, some, high if side else low)
            update(k, h, e, some, applied)

        if k + 1 < STEPS:
            edge(k + 1, h, 1 - side, state[h, e])

    cross_face = diagonal(chip, far)
    cross_sum[...] = jnp.zeros(cross_sum.shape, jnp.float32)
    for k in range(parts):
        if k + 1 == parts:
            for e in range(elements):
                block_copy(1, e, across, across).wait_recv()
                launch(block_copy(2, e, across, partner))
            for e in range(elements):
                block_copy(0, e, partner, partner).wait_recv()
                block_copy(2, e, diagonal_peer, partner).wait_recv()
            for h in range(2):
                for side in range(2):
                    halo(0, h, side).wait_recv()
                held = pl.ds(h * columns, columns)
                for e in range(elements):
                    for q in range(2):
                        some = slice(q * wide, (q + 1) * wide)
                        found = applied_by(e, some, q * wide, wide, vectors[e, some, held])
                        out[e, some, held] = found + through(0, h, e, some, slice(0, 4 * faced))
        for other in range(2):
            side = lax.rem(core + other, 2)
            send(
                basis.at[far, k, :, aligned(core, half)],
                cross.at[k, aligned(side, rows)],
                cross_send.at[other, k],
                cross_recv.at[other, k],
                inner=far * 2 + side,
            ).wait_recv()
        weighted(
            pl.ds(chip, 1), pl.ds(chip, 1), own.at[chip, k], cross.at[k], k, cross_sum, False
        )
    final = send(
        cross_sum.at[aligned(1 - core, rows)],
        cross_other,
        sum_send.at[elements],
        sum_recv.at[elements],
        inner=partner,
    )
    launch(final)
    final.wait_recv()
    gram = (cross_sum[aligned(core, rows)] + cross_other[...]) / grid
    block_of(chip, me, far)[...] = (gram + cross_face).astype(jnp.bfloat16)
    for d, peer in enumerate(sources):
        launch(block_copy(d, elements, me, peer))
    for d, source in enumerate(sources):
        block_copy(d, elements, source, source).wait_recv()
    for e in range(elements):
        mine, theirs = e * wide, (1 - e) * wide
        found = operator[e, mine : mine + wide, theirs : theirs + wide]
        operator[e, theirs : theirs + wide, mine : mine + wide] = found.T

    for h in range(2):
        held = pl.ds(h * columns, columns)
        for side in (1, 0):
            e = (elements - 1) * (1 - side)
            for q in range(2):
                some = slice(q * wide, (q + 1) * wide)
                rest = slice((1 - q) * wide, (2 - q) * wide)
                applied = out[e, some, held]
                applied += applied_by(e, some, (1 - q) * wide, wide, vectors[e, rest, held])
                update(0, h, e, some, applied)
            edge(1, h, 1 - side, state[h, e])

    def kept(h):
        return lambda e: state[h, e]

    for h in range(2):
        inside(1, h, kept(h))
        before(1, h)
    for k in range(1, STEPS):
        for h in range(2):
            for side in (1, 0):
                after(k, h, side)
            if k + 1 < STEPS:
                inside(k + 1, h, kept(h))
                before(k + 1, h)

    for copy in sends:
        copy.wait_send()


def fused(inner, ring, basis, potential, face_index, face_match, vectors):
    elements, parts, rows, grid = basis.shape
    total, width = vectors.shape[1], vectors.shape[2]
    faced = face_index.shape[2]
    half = grid // 2
    bf16, f32, dma = jnp.bfloat16, jnp.float32, pltpu.SemaphoreType.DMA
    vmem = pl.BlockSpec(memory_space=pltpu.VMEM)
    return pl.pallas_call(
        functools.partial(assemble_and_filter, inner, ring),
        out_shape=jax.ShapeDtypeStruct(vectors.shape, f32),
        in_specs=[pl.BlockSpec(memory_space=pltpu.HBM)] + [vmem] * 4,
        out_specs=vmem,
        scratch_shapes=[
            pltpu.VMEM((elements, parts, 2 * rows, half), bf16),
            pltpu.VMEM((parts, 2 * rows, half), bf16),
            pltpu.VMEM((elements, 2, rows, grid), bf16),
            pltpu.VMEM((elements, total, 4 * faced), bf16),
            pltpu.VMEM((elements, 4 * faced, total), bf16),
            pltpu.VMEM((elements, total, total), bf16),
            pltpu.VMEM((elements, 2 * rows, 2 * rows), f32),
            pltpu.VMEM((2 * rows, 2 * rows), f32),
            pltpu.VMEM((elements, rows, 2 * rows), f32),
            pltpu.VMEM((rows, 2 * rows), f32),
            pltpu.VMEM((2, elements, total, width // 2), bf16),
            pltpu.VMEM((STEPS, 2, elements, 4 * faced, width // 2), bf16),
            pltpu.VMEM((STEPS, 2, 2, 2 * faced, width // 2), bf16),
            pltpu.VMEM((2, elements, total, width // 2), f32),
            pltpu.VMEM((2, elements, total, width // 2), f32),
            dma((1 + elements, parts)),
            dma((elements, parts)),
            dma((elements, parts)),
            dma((2, parts)),
            dma((2, parts)),
            dma((inner - 1, elements)),
            dma((inner - 1, elements)),
            dma((elements + 1,)),
            dma((elements + 1,)),
            dma((inner - 1, elements + 1)),
            dma((inner - 1, elements + 1)),
            dma((STEPS, 2, 2)),
            dma((STEPS, 2, 2)),
        ],
        compiler_params=pltpu.CompilerParams(
            collective_id=0, has_side_effects=True, vmem_limit_bytes=60 * 1024 * 1024
        ),
    )(basis, potential, face_index, face_match, vectors)


def solution(mesh):
    inner, ring = mesh.shape["inner"], mesh.shape["elem"]
    placed = (
        P("elem", None, "inner", None),
        P("elem", None),
        P("elem", None, None),
        P("elem", None),
        P("elem", None, "inner"),
    )

    def local(basis, *rest):
        if inner == 4 and basis.shape[0] == 2:
            return fused(inner, ring, basis, *rest)
        return per_device(basis, *rest)

    return jax.shard_map(
        local, mesh=mesh, in_specs=placed, out_specs=P("elem", None, "inner"), check_vma=False
    )
```

```python
import functools

import jax
import jax.numpy as jnp
from jax import lax
from jax.experimental import pallas as pl
from jax.experimental.pallas import tpu as pltpu
from jax.sharding import PartitionSpec as P

MESH = pl.DeviceIdType.MESH

NG = 4096
F = 128
STEPS = 6


CENTER = 5.25
HALF_WIDTH = 2.75


def padded_2(cells, sides, width):
    for axis, dim in sides:
        count = lax.axis_size(axis)
        head = lax.slice_in_dim(cells, 0, width, axis=dim)
        tail = lax.slice_in_dim(cells, cells.shape[dim] - width, cells.shape[dim], axis=dim)
        cells = jnp.concatenate(
            [
                lax.ppermute(tail, axis, [(i, (i + 1) % count) for i in range(count)]),
                cells,
                lax.ppermute(head, axis, [((i + 1) % count, i) for i in range(count)]),
            ],
            axis=dim,
        )
    return cells


def chebyshev_norm(count):
    ratio = (CENTER - 1.0) / HALF_WIDTH
    root = ratio + (ratio * ratio - 1.0) ** 0.5
    return 0.5 * (root**count + root ** (-count))


def face_pair(leading, second):
    return jnp.einsum(
        "nsaf,nsbf->nab", leading, jnp.flip(second, 1), preferred_element_type=jnp.float32
    ) / (4.0 * F)


def gram_terms(exchanged):
    scaled = exchanged[:, 0]
    slopes = exchanged[:, 1:4]
    volume = jnp.einsum("nag,nbg->nab", scaled, scaled, preferred_element_type=jnp.float32)
    kinetic = jnp.einsum("ncag,ncbg->nab", slopes, slopes, preferred_element_type=jnp.float32)
    return (volume + 0.5 * kinetic) / NG


def face_values(element_block, element_points):
    return jnp.take(element_block[0:2], element_points, axis=2)


def per_device(basis, potential, face_index, face_match, vectors):
    elements = basis.shape[0]
    scaled = (jnp.sqrt(potential)[:, None, :] * basis[:, 0].astype(jnp.float32)).astype(
        jnp.bfloat16
    )
    grid_pack = jnp.concatenate((scaled[:, None], basis[:, 1:4]), axis=1)
    gram_part = gram_terms(
        lax.all_to_all(grid_pack, "inner", split_axis=3, concat_axis=2, tiled=True)
    )
    left_points = jnp.take_along_axis(face_index[:, 0, :], face_match, axis=1)
    right_found = jax.vmap(face_values)(basis, face_index[:, 1, :])
    left_found = jax.vmap(face_values)(basis, left_points)
    right_flux = (
        0.5 * right_found[:, 0].astype(jnp.float32) - 0.25 * right_found[:, 1].astype(jnp.float32)
    ).astype(jnp.bfloat16)
    left_flux = (
        -0.5 * left_found[:, 0].astype(jnp.float32) - 0.25 * left_found[:, 1].astype(jnp.float32)
    ).astype(jnp.bfloat16)
    right_sides = jnp.stack((right_flux, right_found[:, 0]), axis=1)
    left_sides = jnp.stack((left_flux, -left_found[:, 0]), axis=1)
    rim_sides = jnp.stack((left_sides[0], right_sides[-1]))
    rim_padded = padded_2(rim_sides, (("elem", 0),), 1)
    from_left = rim_padded[0:1]
    from_right = rim_padded[3:4]
    local_sides = jnp.concatenate((right_sides, left_sides, from_left, from_right), axis=0)
    full_sides = lax.all_gather(local_sides, "inner", axis=2, tiled=True)
    full_rights = full_sides[:elements]
    full_lefts = full_sides[elements : 2 * elements]
    full_next = full_sides[2 * elements + 1 : 2 * elements + 2]
    full_prev = full_sides[2 * elements : 2 * elements + 1]
    next_lefts = jnp.concatenate((full_lefts[1:], full_next), axis=0)
    gram_sum = lax.psum(gram_part, "inner")
    diagonal = (
        gram_sum + face_pair(full_rights, full_rights) + face_pair(full_lefts, full_lefts)
    ).astype(jnp.bfloat16)
    upper_blocks = face_pair(full_rights, next_lefts).astype(jnp.bfloat16)
    first_lower = face_pair(full_prev, full_lefts[0:1]).astype(jnp.bfloat16)
    lower_blocks = jnp.concatenate((first_lower, upper_blocks[:-1]), axis=0)

    def apply_operator(current_bf):
        padded = padded_2(current_bf, (("elem", 0),), 1)
        result = jnp.einsum(
            "jab,jbv->jav", diagonal, current_bf, preferred_element_type=jnp.float32
        )
        result = result + jnp.einsum(
            "jab,jbv->jav", upper_blocks, padded[2:], preferred_element_type=jnp.float32
        )
        result = result + jnp.einsum(
            "jba,jbv->jav", lower_blocks, padded[:-2], preferred_element_type=jnp.float32
        )
        return result

    previous = vectors.astype(jnp.float32)
    current = (apply_operator(vectors) - CENTER * previous) / HALF_WIDTH
    for iteration in range(1, STEPS):
        applied = apply_operator(current.astype(jnp.bfloat16))
        following = 2.0 * (applied - CENTER * current) / HALF_WIDTH - previous
        previous = current
        current = following
    return current / chebyshev_norm(STEPS)


def assemble_and_filter(
    inner,
    ring,
    basis,
    potential,
    face_index,
    face_match,
    vectors,
    out,
    own,
    cross,
    nodal,
    faces,
    turned,
    operator,
    own_sum,
    cross_sum,
    own_other,
    cross_other,
    state,
    links,
    edges,
    current,
    previous,
    local_sem,
    pair_send,
    pair_recv,
    cross_send,
    cross_recv,
    face_send,
    face_recv,
    sum_send,
    sum_recv,
    block_send,
    block_recv,
    halo_send,
    halo_recv,
):
    elements, parts, rows, grid = basis.shape
    total = rows * inner
    faced = face_index.shape[2]
    half = grid // 2
    step_k = min(half, 512)
    columns = vectors.shape[2] // 2
    me = lax.axis_index("inner")
    place = lax.axis_index("elem")
    chip, core = me // 2, lax.rem(me, 2)
    partner = chip * 2 + (1 - core)
    far = 1 - chip
    following = lax.rem(place + 1, ring)
    preceding = lax.rem(place + ring - 1, ring)
    peers = [lax.rem(me + d, inner) for d in range(1, inner)]
    across = far * 2 + core
    diagonal_peer = far * 2 + (1 - core)
    routes = ((0, partner), (1, across))
    sources = (partner, across, diagonal_peer)

    def aligned(index, size):
        return pl.ds(pl.multiple_of(index * size, size), size)

    def send(src, dst, send_sem, recv_sem, **where):
        return pltpu.make_async_remote_copy(
            src_ref=src,
            dst_ref=dst,
            send_sem=send_sem,
            recv_sem=recv_sem,
            device_id=where,
            device_id_type=MESH,
        )

    barrier = pltpu.get_barrier_semaphore()
    for peer in peers:
        pl.semaphore_signal(barrier, inc=1, device_id={"inner": peer}, device_id_type=MESH)
    for peer in (preceding, following):
        pl.semaphore_signal(barrier, inc=1, device_id={"elem": peer}, device_id_type=MESH)

    nodal_copy = pltpu.make_async_copy(basis.at[:, 0:2], nodal, local_sem.at[0, 0])
    nodal_copy.start()
    local = {}
    for e in range(elements):
        for k in range(parts):
            local[e, k] = pltpu.make_async_copy(
                basis.at[e, k, :, aligned(core, half)],
                own.at[e, k, aligned(core, rows)],
                local_sem.at[1 + e, k],
            )
            local[e, k].start()

    pl.semaphore_wait(barrier, inner + 1)

    sends = []

    def launch(copy):
        copy.start()
        sends.append(copy)

    def start_cross(k):
        for other in range(2):
            side = lax.rem(core + other, 2)
            launch(
                send(
                    basis.at[far, k, :, aligned(side, half)],
                    cross.at[k, aligned(core, rows)],
                    cross_send.at[other, k],
                    cross_recv.at[other, k],
                    inner=far * 2 + side,
                )
            )

    start_cross(0)
    for e in range(elements):
        for k in range(parts):
            launch(
                send(
                    basis.at[e, k, :, aligned(1 - core, half)],
                    own.at[e, k, aligned(core, rows)],
                    pair_send.at[e, k],
                    pair_recv.at[e, k],
                    inner=partner,
                )
            )

    low, high = pl.ds(0, 2 * faced), pl.ds(2 * faced, 2 * faced)
    turn_side = lax.rem(place, 2)

    def halo(k, h, side):
        return send(
            edges.at[k, h, side],
            links.at[k, h, (elements - 1) * (1 - side), aligned(side, 2 * faced)],
            halo_send.at[k, h, side],
            halo_recv.at[k, h, side],
            elem=lax.rem(place + ring + 2 * side - 1, ring),
        )

    nodal_copy.wait()
    square = (faced, faced)
    for e in range(elements):
        down = lax.broadcasted_iota(jnp.int32, square, 0)
        along = lax.broadcasted_iota(jnp.int32, square, 1)
        left_row = jnp.broadcast_to(face_index[e, 0:1, :], square)
        left_column = jnp.sum(jnp.where(down == along, left_row, 0), axis=1, keepdims=True)
        matched = jnp.broadcast_to(face_match[e : e + 1, :], square) == down
        left_points = jnp.sum(
            jnp.where(matched, jnp.broadcast_to(left_column, square), 0), axis=0, keepdims=True
        )
        points = jnp.concatenate([face_index[e, 1:2, :], left_points], axis=1)

        def pick(index, found, e=e, points=points):
            offset = pl.multiple_of(index * step_k, step_k)
            spots = lax.broadcasted_iota(jnp.int32, (step_k, 2 * faced), 0) + offset
            chosen = (spots == jnp.broadcast_to(points, spots.shape)).astype(jnp.float32)
            chosen = chosen.astype(jnp.bfloat16)
            return tuple(
                found[k]
                + jnp.dot(
                    nodal[e, k, :, pl.ds(offset, step_k)],
                    chosen,
                    preferred_element_type=jnp.float32,
                )
                for k in range(2)
            )

        start = jnp.zeros((rows, 2 * faced), jnp.float32)
        value, slope = lax.fori_loop(0, grid // step_k, pick, (start, start))
        right_value, left_value = value[:, :faced], value[:, faced:]
        right_slope, left_slope = slope[:, :faced], slope[:, faced:]
        mine = aligned(me, rows)
        pieces = (
            0.5 * right_value - 0.25 * right_slope,
            right_value,
            -0.5 * left_value - 0.25 * left_slope,
            -left_value,
        )
        for index, piece in enumerate(pieces):
            faces[e, mine, index * faced : (index + 1) * faced] = piece.astype(jnp.bfloat16)
    def face_copy(d, e, owner, target):
        block = faces.at[e, aligned(owner, rows)]
        return send(block, block, face_send.at[d, e], face_recv.at[d, e], inner=target)

    for d, peer in routes:
        for e in range(elements):
            launch(face_copy(d, e, me, peer))
    for k in range(1, parts - 1):
        start_cross(k)

    def product(left, right):
        return lax.dot_general(
            left, right, (((1,), (1,)), ((), ())), preferred_element_type=jnp.float32
        )

    def swapped(side):
        cut = [side[:, k * faced : (k + 1) * faced] for k in range(side.shape[1] // faced)]
        order = [k + 1 - 2 * (k % 2) for k in range(len(cut))]
        return jnp.concatenate([cut[k] for k in order], axis=1)

    def weighted(row_left, row_right, left, right, k, target, scale_left):
        @pl.loop(0, half // step_k)
        def _(index):
            offset = pl.multiple_of(index * step_k, step_k)
            span = pl.ds(offset, step_k)
            there = pl.ds(pl.multiple_of(core * half + offset, step_k), step_k)
            one = left[:, span]
            if k == 0 and scale_left:
                root = jnp.sqrt(potential[row_left, there])
                one = (one.astype(jnp.float32) * root).astype(jnp.bfloat16)
                left[:, span] = one
            two = one if right is left else right[:, span]
            if k == 0 and right is not left:
                root = jnp.sqrt(potential[row_right, there])
                two = (two.astype(jnp.float32) * root).astype(jnp.bfloat16)
            term = product(one, two)
            target[...] += term if k == 0 else 0.5 * term

    for e in range(elements):
        own_sum[e] = jnp.zeros(own_sum.shape[1:], jnp.float32)
        for k in range(parts):
            local[e, k].wait()
            send(
                basis.at[e, k, :, aligned(core, half)],
                own.at[e, k, aligned(1 - core, rows)],
                pair_send.at[e, k],
                pair_recv.at[e, k],
                inner=partner,
            ).wait_recv()
            block = own.at[e, k]
            weighted(pl.ds(e, 1), pl.ds(e, 1), block, block, k, own_sum.at[e], True)
        launch(
            send(
                own_sum.at[e, aligned(1 - core, rows)],
                own_other.at[e],
                sum_send.at[e],
                sum_recv.at[e],
                inner=partner,
            )
        )

    for e in range(elements):
        face_copy(1, e, across, across).wait_recv()
        launch(face_copy(2, e, across, partner))
    for e in range(elements):
        face_copy(0, e, partner, partner).wait_recv()
        face_copy(2, e, diagonal_peer, partner).wait_recv()
    for e in range(elements):
        for index in range(4):
            cut = faces[e, :, index * faced : (index + 1) * faced]
            turn = index + 1 - 2 * (index % 2)
            turned[e, turn * faced : (turn + 1) * faced, :] = cut.T

    def coupled(e, cut, values):
        found = jnp.dot(turned[e, cut, :], values, preferred_element_type=jnp.float32)
        return (found * (1.0 / (4.0 * faced))).astype(jnp.bfloat16)

    def edge(k, h, side, values):
        edges[k, h, side] = coupled((elements - 1) * side, aligned(1 - side, 2 * faced), values)

    def inside(k, h, of):
        for e in range(elements - 1):
            links[k, h, e, low] = coupled(e + 1, high, of(e + 1))
            links[k, h, e + 1, high] = coupled(e, low, of(e))

    def given(h):
        return lambda e: vectors[e, :, h * columns : (h + 1) * columns]

    for h in range(2):
        for side in range(2):
            edge(0, h, side, given(h)((elements - 1) * side))
            launch(halo(0, h, side))
    for h in range(2):
        inside(0, h, given(h))

    def diagonal(e, to_chip):
        return product(
            faces[e, aligned(me, rows)], swapped(faces[e, aligned(to_chip, 2 * rows)])
        ) / (4.0 * faced)

    def block_of(e, owner, to_chip):
        return operator.at[e, aligned(owner, rows), aligned(to_chip, 2 * rows)]

    def block_copy(d, slot, owner, target):
        owner_chip = owner // 2
        e = slot if slot < elements else owner_chip
        block = block_of(e, owner, owner_chip if slot < elements else 1 - owner_chip)
        return send(
            block, block, block_send.at[d, slot], block_recv.at[d, slot], inner=target
        )

    for e in range(elements):
        send(
            own_sum.at[e, aligned(core, rows)],
            own_other.at[e],
            sum_send.at[e],
            sum_recv.at[e],
            inner=partner,
        ).wait_recv()
        gram = (own_sum[e, aligned(core, rows)] + own_other[e]) / grid
        block_of(e, me, chip)[...] = (gram + diagonal(e, chip)).astype(jnp.bfloat16)
        for d, peer in routes:
            launch(block_copy(d, e, me, peer))
    start_cross(parts - 1)

    for h in range(2):
        for e in range(elements):
            piece = vectors[e, :, h * columns : (h + 1) * columns]
            current[h, e] = piece.astype(jnp.float32)

    norm = chebyshev_norm(STEPS)
    tile = min(total, 256)
    wide = 2 * rows

    def applied_by(e, some, begin, length, values):
        return jnp.dot(
            operator[e, some, begin : begin + length],
            values,
            preferred_element_type=jnp.float32,
        )

    def through(k, h, e, some, cut):
        return jnp.dot(
            faces[e, some, cut], links[k, h, e, cut], preferred_element_type=jnp.float32
        )

    def update(k, h, e, some, applied):
        scale = (2.0 if k else 1.0) / HALF_WIDTH
        now = current[h, e, some]
        moved = scale * applied - (scale * CENTER) * now
        if k:
            moved = moved - previous[h, e, some]
        if k + 1 == STEPS:
            out[e, some, h * columns : (h + 1) * columns] = moved * (1.0 / norm)
        else:
            previous[h, e, some] = now
            current[h, e, some] = moved
            state[h, e, some] = moved.astype(jnp.bfloat16)

    def before(k, h):
        @pl.loop(0, total // tile)
        def _(index):
            some = pl.ds(pl.multiple_of(index * tile, tile), tile)
            for e in range(elements):
                found = applied_by(e, some, 0, total, state[h, e])
                if e:
                    found += through(k, h, e, some, high)
                if e + 1 < elements:
                    found += through(k, h, e, some, low)
                out[e, some, h * columns : (h + 1) * columns] = found

    def after(k, h, side):
        e = (elements - 1) * (1 - side)
        halo(k, h, side).wait_recv()

        @pl.loop(0, total // tile)
        def _(index):
            some = pl.ds(pl.multiple_of(index * tile, tile), tile)
            applied = out[e, some, h * columns : (h + 1) * columns]
            applied += through(k, h, e, some, aligned(side, 2 * faced))
            update(k, h, e, some, applied)

        if k + 1 < STEPS:
            edge(k + 1, h, 1 - side, state[h, e])

    def fire(k, h):
        for side in (turn_side, 1 - turn_side):
            launch(halo(k, h, side))

    cross_face = diagonal(chip, far)
    cross_sum[...] = jnp.zeros(cross_sum.shape, jnp.float32)
    for k in range(parts):
        if k + 1 == parts:
            for e in range(elements):
                block_copy(1, e, across, across).wait_recv()
                launch(block_copy(2, e, across, partner))
            for e in range(elements):
                block_copy(0, e, partner, partner).wait_recv()
                block_copy(2, e, diagonal_peer, partner).wait_recv()
            for h in range(2):
                for side in range(2):
                    halo(0, h, side).wait_recv()
                held = pl.ds(h * columns, columns)
                for e in range(elements):
                    for q in range(2):
                        some = slice(q * wide, (q + 1) * wide)
                        found = applied_by(e, some, q * wide, wide, vectors[e, some, held])
                        out[e, some, held] = found + through(0, h, e, some, slice(0, 4 * faced))
        for other in range(2):
            side = lax.rem(core + other, 2)
            send(
                basis.at[far, k, :, aligned(core, half)],
                cross.at[k, aligned(side, rows)],
                cross_send.at[other, k],
                cross_recv.at[other, k],
                inner=far * 2 + side,
            ).wait_recv()
        weighted(
            pl.ds(chip, 1), pl.ds(chip, 1), own.at[chip, k], cross.at[k], k, cross_sum, False
        )
    final = send(
        cross_sum.at[aligned(1 - core, rows)],
        cross_other,
        sum_send.at[elements],
        sum_recv.at[elements],
        inner=partner,
    )
    launch(final)
    final.wait_recv()
    gram = (cross_sum[aligned(core, rows)] + cross_other[...]) / grid
    block_of(chip, me, far)[...] = (gram + cross_face).astype(jnp.bfloat16)
    for d, peer in enumerate(sources):
        launch(block_copy(d, elements, me, peer))
    for d, source in enumerate(sources):
        block_copy(d, elements, source, source).wait_recv()
    for e in range(elements):
        mine, theirs = e * wide, (1 - e) * wide
        found = operator[e, mine : mine + wide, theirs : theirs + wide]
        operator[e, theirs : theirs + wide, mine : mine + wide] = found.T

    for h in range(2):
        held = pl.ds(h * columns, columns)
        for side in (1, 0):
            e = (elements - 1) * (1 - side)
            for q in range(2):
                some = slice(q * wide, (q + 1) * wide)
                rest = slice((1 - q) * wide, (2 - q) * wide)
                applied = out[e, some, held]
                applied += applied_by(e, some, (1 - q) * wide, wide, vectors[e, rest, held])
                update(0, h, e, some, applied)
            edge(1, h, 1 - side, state[h, e])
        fire(1, h)

    def kept(h):
        return lambda e: state[h, e]

    for h in range(2):
        inside(1, h, kept(h))
        before(1, h)
    for k in range(1, STEPS):
        for h in range(2):
            for side in (1 - turn_side, turn_side):
                after(k, h, side)
                if k + 1 < STEPS:
                    launch(halo(k + 1, h, 1 - side))
            if k + 1 < STEPS:
                inside(k + 1, h, kept(h))
                before(k + 1, h)

    for copy in sends:
        copy.wait_send()


def fused(inner, ring, basis, potential, face_index, face_match, vectors):
    elements, parts, rows, grid = basis.shape
    total, width = vectors.shape[1], vectors.shape[2]
    faced = face_index.shape[2]
    half = grid // 2
    bf16, f32, dma = jnp.bfloat16, jnp.float32, pltpu.SemaphoreType.DMA
    vmem = pl.BlockSpec(memory_space=pltpu.VMEM)
    return pl.pallas_call(
        functools.partial(assemble_and_filter, inner, ring),
        out_shape=pltpu.VMEM(vectors.shape, f32),
        in_specs=[pl.BlockSpec(memory_space=pltpu.HBM)] + [vmem] * 4,
        out_specs=vmem,
        scratch_shapes=[
            pltpu.VMEM((elements, parts, 2 * rows, half), bf16),
            pltpu.VMEM((parts, 2 * rows, half), bf16),
            pltpu.VMEM((elements, 2, rows, grid), bf16),
            pltpu.VMEM((elements, total, 4 * faced), bf16),
            pltpu.VMEM((elements, 4 * faced, total), bf16),
            pltpu.VMEM((elements, total, total), bf16),
            pltpu.VMEM((elements, 2 * rows, 2 * rows), f32),
            pltpu.VMEM((2 * rows, 2 * rows), f32),
            pltpu.VMEM((elements, rows, 2 * rows), f32),
            pltpu.VMEM((rows, 2 * rows), f32),
            pltpu.VMEM((2, elements, total, width // 2), bf16),
            pltpu.VMEM((STEPS, 2, elements, 4 * faced, width // 2), bf16),
            pltpu.VMEM((STEPS, 2, 2, 2 * faced, width // 2), bf16),
            pltpu.VMEM((2, elements, total, width // 2), f32),
            pltpu.VMEM((2, elements, total, width // 2), f32),
            dma((1 + elements, parts)),
            dma((elements, parts)),
            dma((elements, parts)),
            dma((2, parts)),
            dma((2, parts)),
            dma((inner - 1, elements)),
            dma((inner - 1, elements)),
            dma((elements + 1,)),
            dma((elements + 1,)),
            dma((inner - 1, elements + 1)),
            dma((inner - 1, elements + 1)),
            dma((STEPS, 2, 2)),
            dma((STEPS, 2, 2)),
        ],
        compiler_params=pltpu.CompilerParams(
            collective_id=0, has_side_effects=True, vmem_limit_bytes=60 * 1024 * 1024
        ),
    )(basis, potential, face_index, face_match, vectors)


def solution(mesh):
    inner, ring = mesh.shape["inner"], mesh.shape["elem"]
    placed = (
        P("elem", None, "inner", None),
        P("elem", None),
        P("elem", None, None),
        P("elem", None),
        P("elem", None, "inner"),
    )

    def local(basis, *rest):
        if inner == 4 and basis.shape[0] == 2:
            return fused(inner, ring, basis, *rest)
        return per_device(basis, *rest)

    return jax.shard_map(
        local, mesh=mesh, in_specs=placed, out_specs=P("elem", None, "inner"), check_vma=False
    )
```

```python
import functools

import jax
import jax.numpy as jnp
from jax import lax
from jax.experimental import pallas as pl
from jax.experimental.pallas import tpu as pltpu
from jax.sharding import PartitionSpec as P

MESH = pl.DeviceIdType.MESH

NG = 4096
F = 128
STEPS = 6


CENTER = 5.25
HALF_WIDTH = 2.75


def padded_2(cells, sides, width):
    for axis, dim in sides:
        count = lax.axis_size(axis)
        head = lax.slice_in_dim(cells, 0, width, axis=dim)
        tail = lax.slice_in_dim(cells, cells.shape[dim] - width, cells.shape[dim], axis=dim)
        cells = jnp.concatenate(
            [
                lax.ppermute(tail, axis, [(i, (i + 1) % count) for i in range(count)]),
                cells,
                lax.ppermute(head, axis, [((i + 1) % count, i) for i in range(count)]),
            ],
            axis=dim,
        )
    return cells


def chebyshev_norm(count):
    ratio = (CENTER - 1.0) / HALF_WIDTH
    root = ratio + (ratio * ratio - 1.0) ** 0.5
    return 0.5 * (root**count + root ** (-count))


def face_pair(leading, second):
    return jnp.einsum(
        "nsaf,nsbf->nab", leading, jnp.flip(second, 1), preferred_element_type=jnp.float32
    ) / (4.0 * F)


def gram_terms(exchanged):
    scaled = exchanged[:, 0]
    slopes = exchanged[:, 1:4]
    volume = jnp.einsum("nag,nbg->nab", scaled, scaled, preferred_element_type=jnp.float32)
    kinetic = jnp.einsum("ncag,ncbg->nab", slopes, slopes, preferred_element_type=jnp.float32)
    return (volume + 0.5 * kinetic) / NG


def face_values(element_block, element_points):
    return jnp.take(element_block[0:2], element_points, axis=2)


def per_device(basis, potential, face_index, face_match, vectors):
    elements = basis.shape[0]
    scaled = (jnp.sqrt(potential)[:, None, :] * basis[:, 0].astype(jnp.float32)).astype(
        jnp.bfloat16
    )
    grid_pack = jnp.concatenate((scaled[:, None], basis[:, 1:4]), axis=1)
    gram_part = gram_terms(
        lax.all_to_all(grid_pack, "inner", split_axis=3, concat_axis=2, tiled=True)
    )
    left_points = jnp.take_along_axis(face_index[:, 0, :], face_match, axis=1)
    right_found = jax.vmap(face_values)(basis, face_index[:, 1, :])
    left_found = jax.vmap(face_values)(basis, left_points)
    right_flux = (
        0.5 * right_found[:, 0].astype(jnp.float32) - 0.25 * right_found[:, 1].astype(jnp.float32)
    ).astype(jnp.bfloat16)
    left_flux = (
        -0.5 * left_found[:, 0].astype(jnp.float32) - 0.25 * left_found[:, 1].astype(jnp.float32)
    ).astype(jnp.bfloat16)
    right_sides = jnp.stack((right_flux, right_found[:, 0]), axis=1)
    left_sides = jnp.stack((left_flux, -left_found[:, 0]), axis=1)
    rim_sides = jnp.stack((left_sides[0], right_sides[-1]))
    rim_padded = padded_2(rim_sides, (("elem", 0),), 1)
    from_left = rim_padded[0:1]
    from_right = rim_padded[3:4]
    local_sides = jnp.concatenate((right_sides, left_sides, from_left, from_right), axis=0)
    full_sides = lax.all_gather(local_sides, "inner", axis=2, tiled=True)
    full_rights = full_sides[:elements]
    full_lefts = full_sides[elements : 2 * elements]
    full_next = full_sides[2 * elements + 1 : 2 * elements + 2]
    full_prev = full_sides[2 * elements : 2 * elements + 1]
    next_lefts = jnp.concatenate((full_lefts[1:], full_next), axis=0)
    gram_sum = lax.psum(gram_part, "inner")
    diagonal = (
        gram_sum + face_pair(full_rights, full_rights) + face_pair(full_lefts, full_lefts)
    ).astype(jnp.bfloat16)
    upper_blocks = face_pair(full_rights, next_lefts).astype(jnp.bfloat16)
    first_lower = face_pair(full_prev, full_lefts[0:1]).astype(jnp.bfloat16)
    lower_blocks = jnp.concatenate((first_lower, upper_blocks[:-1]), axis=0)

    def apply_operator(current_bf):
        padded = padded_2(current_bf, (("elem", 0),), 1)
        result = jnp.einsum(
            "jab,jbv->jav", diagonal, current_bf, preferred_element_type=jnp.float32
        )
        result = result + jnp.einsum(
            "jab,jbv->jav", upper_blocks, padded[2:], preferred_element_type=jnp.float32
        )
        result = result + jnp.einsum(
            "jba,jbv->jav", lower_blocks, padded[:-2], preferred_element_type=jnp.float32
        )
        return result

    previous = vectors.astype(jnp.float32)
    current = (apply_operator(vectors) - CENTER * previous) / HALF_WIDTH
    for iteration in range(1, STEPS):
        applied = apply_operator(current.astype(jnp.bfloat16))
        following = 2.0 * (applied - CENTER * current) / HALF_WIDTH - previous
        previous = current
        current = following
    return current / chebyshev_norm(STEPS)


def assemble_and_filter(
    inner,
    ring,
    basis,
    potential_in,
    face_index_in,
    face_match_in,
    vectors_in,
    out,
    potential,
    face_index,
    face_match,
    vectors,
    found,
    found_mine,
    found_other,
    own,
    cross,
    nodal,
    faces,
    turned,
    operator,
    own_sum,
    cross_sum,
    cross_face,
    own_other,
    cross_other,
    state,
    links,
    edges,
    current,
    previous,
    input_sem,
    local_sem,
    pair_send,
    pair_recv,
    cross_send,
    cross_recv,
    face_send,
    face_recv,
    sum_send,
    sum_recv,
    block_send,
    block_recv,
    halo_send,
    halo_recv,
):
    elements, parts, rows, grid = basis.shape
    total = rows * inner
    faced = face_index.shape[2]
    half = grid // 2
    step_k = min(half, 512)
    columns = vectors.shape[2] // 2
    me = lax.axis_index("inner")
    place = lax.axis_index("elem")
    chip, core = me // 2, lax.rem(me, 2)
    partner = chip * 2 + (1 - core)
    far = 1 - chip
    following = lax.rem(place + 1, ring)
    preceding = lax.rem(place + ring - 1, ring)
    peers = [lax.rem(me + d, inner) for d in range(1, inner)]
    across = far * 2 + core
    diagonal_peer = far * 2 + (1 - core)
    routes = ((0, partner), (1, across))
    sources = (partner, across, diagonal_peer)

    def aligned(index, size):
        return pl.ds(pl.multiple_of(index * size, size), size)

    def send(src, dst, send_sem, recv_sem, **where):
        return pltpu.make_async_remote_copy(
            src_ref=src,
            dst_ref=dst,
            send_sem=send_sem,
            recv_sem=recv_sem,
            device_id=where,
            device_id_type=MESH,
        )

    pieces = [(k, 0, half) for k in range(parts - 1)]
    pieces += [(parts - 1, begin, step_k) for begin in range(0, half, step_k)]

    barrier = pltpu.get_barrier_semaphore()
    for peer in peers:
        pl.semaphore_signal(barrier, inc=1, device_id={"inner": peer}, device_id_type=MESH)
    for peer in (preceding, following):
        pl.semaphore_signal(barrier, inc=1, device_id={"elem": peer}, device_id_type=MESH)

    nodal_copy = pltpu.make_async_copy(basis.at[:, 0:2], nodal, local_sem.at[0, 0])
    nodal_copy.start()
    moved_in = [
        pltpu.make_async_copy(source, target, input_sem.at[index])
        for index, (source, target) in enumerate(
            (
                (potential_in, potential),
                (face_index_in, face_index),
                (face_match_in, face_match),
                (vectors_in, vectors),
            )
        )
    ]
    for copy in moved_in:
        copy.start()
    local = {}
    for e in range(elements):
        for k in range(parts):
            local[e, k] = pltpu.make_async_copy(
                basis.at[e, k, :, aligned(core, half)],
                own.at[e, k, aligned(core, rows)],
                local_sem.at[1 + e, k],
            )
            local[e, k].start()

    pl.semaphore_wait(barrier, inner + 1)

    sends = []

    def launch(copy):
        copy.start()
        sends.append(copy)

    def cross_copy(piece, other):
        k, begin, size = pieces[piece]
        side = lax.rem(core + other, 2)
        return send(
            basis.at[far, k, :, pl.ds(pl.multiple_of(side * half + begin, step_k), size)],
            cross.at[k, aligned(core, rows), begin : begin + size],
            cross_send.at[other, piece],
            cross_recv.at[other, piece],
            inner=far * 2 + side,
        )

    def cross_wait(piece):
        k, begin, size = pieces[piece]
        for other in range(2):
            side = lax.rem(core + other, 2)
            send(
                basis.at[far, k, :, pl.ds(pl.multiple_of(core * half + begin, step_k), size)],
                cross.at[k, aligned(side, rows), begin : begin + size],
                cross_send.at[other, piece],
                cross_recv.at[other, piece],
                inner=far * 2 + side,
            ).wait_recv()

    def start_cross(wanted):
        for piece, (k, _, _) in enumerate(pieces):
            if k == wanted:
                for other in range(2):
                    launch(cross_copy(piece, other))

    start_cross(0)
    for e in range(elements):
        for k in range(parts):
            launch(
                send(
                    basis.at[e, k, :, aligned(1 - core, half)],
                    own.at[e, k, aligned(core, rows)],
                    pair_send.at[e, k],
                    pair_recv.at[e, k],
                    inner=partner,
                )
            )

    low, high = pl.ds(0, 2 * faced), pl.ds(2 * faced, 2 * faced)
    turn_side = lax.rem(place, 2)

    def halo(k, h, side):
        return send(
            edges.at[k, h, side],
            links.at[k, h, (elements - 1) * (1 - side), aligned(side, 2 * faced)],
            halo_send.at[k, h, side],
            halo_recv.at[k, h, side],
            elem=lax.rem(place + ring + 2 * side - 1, ring),
        )

    for copy in moved_in:
        copy.wait()
    nodal_copy.wait()

    def points_of(e):
        square = (faced, faced)
        down = lax.broadcasted_iota(jnp.int32, square, 0)
        along = lax.broadcasted_iota(jnp.int32, square, 1)
        left_row = jnp.broadcast_to(face_index[e, 0:1, :], square)
        left_column = jnp.sum(jnp.where(down == along, left_row, 0), axis=1, keepdims=True)
        matched = jnp.broadcast_to(face_match[pl.ds(e, 1), :], square) == down
        left_points = jnp.sum(
            jnp.where(matched, jnp.broadcast_to(left_column, square), 0), axis=0, keepdims=True
        )
        return jnp.concatenate([face_index[e, 1:2, :], left_points], axis=1)

    def chosen_at(points, offset):
        spots = lax.broadcasted_iota(jnp.int32, (step_k, 2 * faced), 0) + offset
        chosen = (spots == jnp.broadcast_to(points, spots.shape)).astype(jnp.float32)
        return chosen.astype(jnp.bfloat16)

    def write_faces(e, where, value, slope):
        right_value, left_value = value[:, :faced], value[:, faced:]
        right_slope, left_slope = slope[:, :faced], slope[:, faced:]
        sides = (
            0.5 * right_value - 0.25 * right_slope,
            right_value,
            -0.5 * left_value - 0.25 * left_slope,
            -left_value,
        )
        for index, side in enumerate(sides):
            faces[e, where, index * faced : (index + 1) * faced] = side.astype(jnp.bfloat16)

    for e in range(elements):
        points = points_of(e)

        def pick(index, values, e=e, points=points):
            offset = pl.multiple_of(index * step_k, step_k)
            chosen = chosen_at(points, offset)
            return tuple(
                values[k]
                + jnp.dot(
                    nodal[e, k, :, pl.ds(offset, step_k)],
                    chosen,
                    preferred_element_type=jnp.float32,
                )
                for k in range(2)
            )

        start = jnp.zeros((rows, 2 * faced), jnp.float32)
        value, slope = lax.fori_loop(0, grid // step_k, pick, (start, start))
        write_faces(e, aligned(me, rows), value, slope)

    def face_copy(d, slot, e, owner, target):
        block = faces.at[e, aligned(owner, rows)]
        return send(block, block, face_send.at[d, slot], face_recv.at[d, slot], inner=target)

    for e in range(elements):
        launch(face_copy(0, e, e, me, partner))
    launch(face_copy(1, 0, chip, me, across))
    for k in range(1, parts - 1):
        start_cross(k)

    def product(left, right):
        return lax.dot_general(
            left, right, (((1,), (1,)), ((), ())), preferred_element_type=jnp.float32
        )

    def swapped(side):
        cut = [side[:, k * faced : (k + 1) * faced] for k in range(side.shape[1] // faced)]
        order = [k + 1 - 2 * (k % 2) for k in range(len(cut))]
        return jnp.concatenate([cut[k] for k in order], axis=1)

    def weighted(row_left, row_right, left, right, k, target, scale_left, begin=0, size=half):
        @pl.loop(0, size // step_k)
        def _(index):
            offset = pl.multiple_of(begin + index * step_k, step_k)
            span = pl.ds(offset, step_k)
            there = pl.ds(pl.multiple_of(core * half + offset, step_k), step_k)
            one = left[:, span]
            if k == 0 and scale_left:
                root = jnp.sqrt(potential[row_left, there])
                one = (one.astype(jnp.float32) * root).astype(jnp.bfloat16)
                left[:, span] = one
            two = one if right is left else right[:, span]
            if k == 0 and right is not left:
                root = jnp.sqrt(potential[row_right, there])
                two = (two.astype(jnp.float32) * root).astype(jnp.bfloat16)
            term = product(one, two)
            target[...] += term if k == 0 else 0.5 * term

    for e in range(elements):
        own_sum[e] = jnp.zeros(own_sum.shape[1:], jnp.float32)
        for k in range(parts):
            local[e, k].wait()
            send(
                basis.at[e, k, :, aligned(core, half)],
                own.at[e, k, aligned(1 - core, rows)],
                pair_send.at[e, k],
                pair_recv.at[e, k],
                inner=partner,
            ).wait_recv()
            block = own.at[e, k]
            weighted(pl.ds(e, 1), pl.ds(e, 1), block, block, k, own_sum.at[e], True)
        launch(
            send(
                own_sum.at[e, aligned(1 - core, rows)],
                own_other.at[e],
                sum_send.at[e],
                sum_recv.at[e],
                inner=partner,
            )
        )

    for e in range(elements):
        face_copy(0, e, e, partner, partner).wait_recv()

    def diagonal(e, to_chip):
        return product(
            faces[e, aligned(me, rows)], swapped(faces[e, aligned(to_chip, 2 * rows)])
        ) / (4.0 * faced)

    def block_of(e, owner, to_chip):
        return operator.at[e, aligned(owner, rows), aligned(to_chip, 2 * rows)]

    def block_copy(d, slot, owner, target):
        owner_chip = owner // 2
        e = slot if slot < elements else owner_chip
        block = block_of(e, owner, owner_chip if slot < elements else 1 - owner_chip)
        return send(
            block, block, block_send.at[d, slot], block_recv.at[d, slot], inner=target
        )

    for e in range(elements):
        send(
            own_sum.at[e, aligned(core, rows)],
            own_other.at[e],
            sum_send.at[e],
            sum_recv.at[e],
            inner=partner,
        ).wait_recv()
        gram = (own_sum[e, aligned(core, rows)] + own_other[e]) / grid
        block_of(e, me, chip)[...] = (gram + diagonal(e, chip)).astype(jnp.bfloat16)
        for d, peer in routes:
            launch(block_copy(d, e, me, peer))
    start_cross(parts - 1)

    for h in range(2):
        for e in range(elements):
            piece = vectors[e, :, h * columns : (h + 1) * columns]
            current[h, e] = piece.astype(jnp.float32)

    norm = chebyshev_norm(STEPS)
    tile = min(total, 256)
    wide = 2 * rows

    def applied_by(e, some, begin, length, values):
        return jnp.dot(
            operator[e, some, begin : begin + length],
            values,
            preferred_element_type=jnp.float32,
        )

    def through(k, h, e, some, cut):
        return jnp.dot(
            faces[e, some, cut], links[k, h, e, cut], preferred_element_type=jnp.float32
        )

    def update(k, h, e, some, applied):
        scale = (2.0 if k else 1.0) / HALF_WIDTH
        now = current[h, e, some]
        moved = scale * applied - (scale * CENTER) * now
        if k:
            moved = moved - previous[h, e, some]
        if k + 1 == STEPS:
            out[e, some, h * columns : (h + 1) * columns] = moved * (1.0 / norm)
        else:
            previous[h, e, some] = now
            current[h, e, some] = moved
            state[h, e, some] = moved.astype(jnp.bfloat16)

    def before(k, h):
        @pl.loop(0, total // tile)
        def _(index):
            some = pl.ds(pl.multiple_of(index * tile, tile), tile)
            for e in range(elements):
                found = applied_by(e, some, 0, total, state[h, e])
                if e:
                    found += through(k, h, e, some, high)
                if e + 1 < elements:
                    found += through(k, h, e, some, low)
                out[e, some, h * columns : (h + 1) * columns] = found

    def after(k, h, side):
        e = (elements - 1) * (1 - side)
        halo(k, h, side).wait_recv()

        @pl.loop(0, total // tile)
        def _(index):
            some = pl.ds(pl.multiple_of(index * tile, tile), tile)
            applied = out[e, some, h * columns : (h + 1) * columns]
            applied += through(k, h, e, some, aligned(side, 2 * faced))
            update(k, h, e, some, applied)

        if k + 1 < STEPS:
            edge(k + 1, h, 1 - side, state[h, e])

    def coupled(e, cut, values):
        found = jnp.dot(turned[e, cut, :], values, preferred_element_type=jnp.float32)
        return (found * (1.0 / (4.0 * faced))).astype(jnp.bfloat16)

    def edge(k, h, side, values):
        edges[k, h, side] = coupled((elements - 1) * side, aligned(1 - side, 2 * faced), values)

    def inside(k, h, of):
        for e in range(elements - 1):
            links[k, h, e, low] = coupled(e + 1, high, of(e + 1))
            links[k, h, e + 1, high] = coupled(e, low, of(e))

    def given(h):
        return lambda e: vectors[e, :, h * columns : (h + 1) * columns]

    def far_faces():
        points = points_of(chip)
        found[...] = jnp.zeros(found.shape, jnp.float32)

        @pl.loop(0, half // step_k)
        def _(index):
            offset = pl.multiple_of(index * step_k, step_k)
            chosen = chosen_at(points, core * half + offset)
            for k in range(2):
                found[k] += jnp.dot(
                    cross[k, :, pl.ds(offset, step_k)],
                    chosen,
                    preferred_element_type=jnp.float32,
                )

        found_mine[...] = found[...].astype(jnp.bfloat16)
        swap = send(
            found_mine, found_other, face_send.at[1, 1], face_recv.at[1, 1], inner=partner
        )
        launch(swap)
        face_copy(1, 0, far, across, across).wait_recv()
        launch(face_copy(2, 0, far, across, partner))
        swap.wait_recv()
        value, slope = (found[k] + found_other[k].astype(jnp.float32) for k in range(2))
        write_faces(chip, aligned(far, 2 * rows), value, slope)
        face_copy(2, 0, far, diagonal_peer, partner).wait_recv()

    def first_partial():
        for e in range(elements):
            block_copy(1, e, across, across).wait_recv()
            launch(block_copy(2, e, across, partner))
        for e in range(elements):
            block_copy(0, e, partner, partner).wait_recv()
            block_copy(2, e, diagonal_peer, partner).wait_recv()
        for h in range(2):
            for side in range(2):
                halo(0, h, side).wait_recv()
            held = pl.ds(h * columns, columns)
            for e in range(elements):
                for q in range(2):
                    some = slice(q * wide, (q + 1) * wide)
                    value = applied_by(e, some, q * wide, wide, vectors[e, some, held])
                    out[e, some, held] = value + through(0, h, e, some, slice(0, 4 * faced))

    cross_sum[...] = jnp.zeros(cross_sum.shape, jnp.float32)
    for piece, (k, begin, size) in enumerate(pieces):
        if k + 1 == parts and not begin:
            first_partial()
        cross_wait(piece)
        weighted(
            pl.ds(chip, 1),
            pl.ds(chip, 1),
            own.at[chip, k],
            cross.at[k],
            k,
            cross_sum,
            False,
            begin,
            size,
        )
        if k == 1:
            far_faces()
            for e in range(elements):
                for index in range(4):
                    cut = faces[e, :, index * faced : (index + 1) * faced]
                    turn = index + 1 - 2 * (index % 2)
                    turned[e, turn * faced : (turn + 1) * faced, :] = cut.T
            for h in range(2):
                for side in range(2):
                    edge(0, h, side, given(h)((elements - 1) * side))
                    launch(halo(0, h, side))
            for h in range(2):
                inside(0, h, given(h))
            cross_face[...] = diagonal(chip, far)
    final = send(
        cross_sum.at[aligned(1 - core, rows)],
        cross_other,
        sum_send.at[elements],
        sum_recv.at[elements],
        inner=partner,
    )
    launch(final)
    final.wait_recv()
    gram = (cross_sum[aligned(core, rows)] + cross_other[...]) / grid
    block_of(chip, me, far)[...] = (gram + cross_face[...]).astype(jnp.bfloat16)
    for d in (1, 2, 0):
        launch(block_copy(d, elements, me, sources[d]))

    def finish(e):
        mine, theirs = aligned(e, wide), aligned(1 - e, wide)
        operator[e, theirs, mine] = operator[e, mine, theirs].T
        for h in range(2):
            held = pl.ds(h * columns, columns)
            for q in range(2):
                some = slice(q * wide, (q + 1) * wide)
                rest = slice((1 - q) * wide, (2 - q) * wide)
                applied = out[e, some, held]
                applied += applied_by(e, some, (1 - q) * wide, wide, vectors[e, rest, held])
                update(0, h, e, some, applied)
            edge(1, h, e, state[h, e])
            launch(halo(1, h, e))

    block_copy(0, elements, partner, partner).wait_recv()
    finish(chip)
    for d in (1, 2):
        block_copy(d, elements, sources[d], sources[d]).wait_recv()
    finish(far)

    def kept(h):
        return lambda e: state[h, e]

    for h in range(2):
        inside(1, h, kept(h))
        before(1, h)
    for k in range(1, STEPS):
        for h in range(2):
            for side in (1 - turn_side, turn_side):
                after(k, h, side)
                if k + 1 < STEPS:
                    launch(halo(k + 1, h, 1 - side))
            if k + 1 < STEPS:
                inside(k + 1, h, kept(h))
                before(k + 1, h)

    for copy in sends:
        copy.wait_send()


def fused(inner, ring, basis, potential, face_index, face_match, vectors):
    elements, parts, rows, grid = basis.shape
    total, width = vectors.shape[1], vectors.shape[2]
    faced = face_index.shape[2]
    half = grid // 2
    pieces = parts - 1 + half // min(half, 512)
    bf16, f32, dma = jnp.bfloat16, jnp.float32, pltpu.SemaphoreType.DMA
    vmem = pl.BlockSpec(memory_space=pltpu.VMEM)
    return pl.pallas_call(
        functools.partial(assemble_and_filter, inner, ring),
        out_shape=pltpu.VMEM(vectors.shape, f32),
        in_specs=[pl.BlockSpec(memory_space=pltpu.HBM)] * 5,
        out_specs=vmem,
        scratch_shapes=[
            pltpu.VMEM(potential.shape, f32),
            pltpu.VMEM(face_index.shape, jnp.int32),
            pltpu.VMEM(face_match.shape, jnp.int32),
            pltpu.VMEM(vectors.shape, bf16),
            pltpu.VMEM((2, 2 * rows, 2 * faced), f32),
            pltpu.VMEM((2, 2 * rows, 2 * faced), bf16),
            pltpu.VMEM((2, 2 * rows, 2 * faced), bf16),
            pltpu.VMEM((elements, parts, 2 * rows, half), bf16),
            pltpu.VMEM((parts, 2 * rows, half), bf16),
            pltpu.VMEM((elements, 2, rows, grid), bf16),
            pltpu.VMEM((elements, total, 4 * faced), bf16),
            pltpu.VMEM((elements, 4 * faced, total), bf16),
            pltpu.VMEM((elements, total, total), bf16),
            pltpu.VMEM((elements, 2 * rows, 2 * rows), f32),
            pltpu.VMEM((2 * rows, 2 * rows), f32),
            pltpu.VMEM((rows, 2 * rows), f32),
            pltpu.VMEM((elements, rows, 2 * rows), f32),
            pltpu.VMEM((rows, 2 * rows), f32),
            pltpu.VMEM((2, elements, total, width // 2), bf16),
            pltpu.VMEM((STEPS, 2, elements, 4 * faced, width // 2), bf16),
            pltpu.VMEM((STEPS, 2, 2, 2 * faced, width // 2), bf16),
            pltpu.VMEM((2, elements, total, width // 2), f32),
            pltpu.VMEM((2, elements, total, width // 2), f32),
            dma((4,)),
            dma((1 + elements, parts)),
            dma((elements, parts)),
            dma((elements, parts)),
            dma((2, pieces)),
            dma((2, pieces)),
            dma((inner - 1, elements)),
            dma((inner - 1, elements)),
            dma((elements + 1,)),
            dma((elements + 1,)),
            dma((inner - 1, elements + 1)),
            dma((inner - 1, elements + 1)),
            dma((STEPS, 2, 2)),
            dma((STEPS, 2, 2)),
        ],
        compiler_params=pltpu.CompilerParams(
            collective_id=0, has_side_effects=True, vmem_limit_bytes=60 * 1024 * 1024
        ),
    )(basis, potential, face_index, face_match, vectors)


def solution(mesh):
    inner, ring = mesh.shape["inner"], mesh.shape["elem"]
    placed = (
        P("elem", None, "inner", None),
        P("elem", None),
        P("elem", None, None),
        P("elem", None),
        P("elem", None, "inner"),
    )

    def local(basis, *rest):
        if inner == 4 and basis.shape[0] == 2:
            return fused(inner, ring, basis, *rest)
        return per_device(basis, *rest)

    return jax.shard_map(
        local, mesh=mesh, in_specs=placed, out_specs=P("elem", None, "inner"), check_vma=False
    )
```

```python
import functools

import jax
import jax.numpy as jnp
from jax import lax
from jax.experimental import pallas as pl
from jax.experimental.pallas import tpu as pltpu
from jax.sharding import PartitionSpec as P

MESH = pl.DeviceIdType.MESH

NG = 4096
F = 128
STEPS = 6


CENTER = 5.25
HALF_WIDTH = 2.75


def padded_2(cells, sides, width):
    for axis, dim in sides:
        count = lax.axis_size(axis)
        head = lax.slice_in_dim(cells, 0, width, axis=dim)
        tail = lax.slice_in_dim(cells, cells.shape[dim] - width, cells.shape[dim], axis=dim)
        cells = jnp.concatenate(
            [
                lax.ppermute(tail, axis, [(i, (i + 1) % count) for i in range(count)]),
                cells,
                lax.ppermute(head, axis, [((i + 1) % count, i) for i in range(count)]),
            ],
            axis=dim,
        )
    return cells


def chebyshev_norm(count):
    ratio = (CENTER - 1.0) / HALF_WIDTH
    root = ratio + (ratio * ratio - 1.0) ** 0.5
    return 0.5 * (root**count + root ** (-count))


def face_pair(leading, second):
    return jnp.einsum(
        "nsaf,nsbf->nab", leading, jnp.flip(second, 1), preferred_element_type=jnp.float32
    ) / (4.0 * F)


def gram_terms(exchanged):
    scaled = exchanged[:, 0]
    slopes = exchanged[:, 1:4]
    volume = jnp.einsum("nag,nbg->nab", scaled, scaled, preferred_element_type=jnp.float32)
    kinetic = jnp.einsum("ncag,ncbg->nab", slopes, slopes, preferred_element_type=jnp.float32)
    return (volume + 0.5 * kinetic) / NG


def face_values(element_block, element_points):
    return jnp.take(element_block[0:2], element_points, axis=2)


def per_device(basis, potential, face_index, face_match, vectors):
    elements = basis.shape[0]
    scaled = (jnp.sqrt(potential)[:, None, :] * basis[:, 0].astype(jnp.float32)).astype(
        jnp.bfloat16
    )
    grid_pack = jnp.concatenate((scaled[:, None], basis[:, 1:4]), axis=1)
    gram_part = gram_terms(
        lax.all_to_all(grid_pack, "inner", split_axis=3, concat_axis=2, tiled=True)
    )
    left_points = jnp.take_along_axis(face_index[:, 0, :], face_match, axis=1)
    right_found = jax.vmap(face_values)(basis, face_index[:, 1, :])
    left_found = jax.vmap(face_values)(basis, left_points)
    right_flux = (
        0.5 * right_found[:, 0].astype(jnp.float32) - 0.25 * right_found[:, 1].astype(jnp.float32)
    ).astype(jnp.bfloat16)
    left_flux = (
        -0.5 * left_found[:, 0].astype(jnp.float32) - 0.25 * left_found[:, 1].astype(jnp.float32)
    ).astype(jnp.bfloat16)
    right_sides = jnp.stack((right_flux, right_found[:, 0]), axis=1)
    left_sides = jnp.stack((left_flux, -left_found[:, 0]), axis=1)
    rim_sides = jnp.stack((left_sides[0], right_sides[-1]))
    rim_padded = padded_2(rim_sides, (("elem", 0),), 1)
    from_left = rim_padded[0:1]
    from_right = rim_padded[3:4]
    local_sides = jnp.concatenate((right_sides, left_sides, from_left, from_right), axis=0)
    full_sides = lax.all_gather(local_sides, "inner", axis=2, tiled=True)
    full_rights = full_sides[:elements]
    full_lefts = full_sides[elements : 2 * elements]
    full_next = full_sides[2 * elements + 1 : 2 * elements + 2]
    full_prev = full_sides[2 * elements : 2 * elements + 1]
    next_lefts = jnp.concatenate((full_lefts[1:], full_next), axis=0)
    gram_sum = lax.psum(gram_part, "inner")
    diagonal = (
        gram_sum + face_pair(full_rights, full_rights) + face_pair(full_lefts, full_lefts)
    ).astype(jnp.bfloat16)
    upper_blocks = face_pair(full_rights, next_lefts).astype(jnp.bfloat16)
    first_lower = face_pair(full_prev, full_lefts[0:1]).astype(jnp.bfloat16)
    lower_blocks = jnp.concatenate((first_lower, upper_blocks[:-1]), axis=0)

    def apply_operator(current_bf):
        padded = padded_2(current_bf, (("elem", 0),), 1)
        result = jnp.einsum(
            "jab,jbv->jav", diagonal, current_bf, preferred_element_type=jnp.float32
        )
        result = result + jnp.einsum(
            "jab,jbv->jav", upper_blocks, padded[2:], preferred_element_type=jnp.float32
        )
        result = result + jnp.einsum(
            "jba,jbv->jav", lower_blocks, padded[:-2], preferred_element_type=jnp.float32
        )
        return result

    previous = vectors.astype(jnp.float32)
    current = (apply_operator(vectors) - CENTER * previous) / HALF_WIDTH
    for iteration in range(1, STEPS):
        applied = apply_operator(current.astype(jnp.bfloat16))
        following = 2.0 * (applied - CENTER * current) / HALF_WIDTH - previous
        previous = current
        current = following
    return current / chebyshev_norm(STEPS)


def assemble_and_filter(
    inner,
    ring,
    basis,
    potential_in,
    face_index_in,
    face_match_in,
    vectors_in,
    out,
    potential,
    face_index,
    face_match,
    vectors,
    found,
    found_mine,
    found_other,
    own,
    cross,
    nodal,
    faces,
    turned,
    operator,
    own_sum,
    cross_sum,
    cross_face,
    own_other,
    cross_other,
    state,
    links,
    edges,
    current,
    previous,
    input_sem,
    local_sem,
    pair_send,
    pair_recv,
    cross_send,
    cross_recv,
    face_send,
    face_recv,
    sum_send,
    sum_recv,
    block_send,
    block_recv,
    halo_send,
    halo_recv,
    token,
):
    elements, parts, rows, grid = basis.shape
    total = rows * inner
    faced = face_index.shape[2]
    half = grid // 2
    step_k = min(half, 512)
    columns = vectors.shape[2] // 2
    me = lax.axis_index("inner")
    place = lax.axis_index("elem")
    chip, core = me // 2, lax.rem(me, 2)
    partner = chip * 2 + (1 - core)
    far = 1 - chip
    peers = [lax.rem(me + d, inner) for d in range(1, inner)]
    across = far * 2 + core
    diagonal_peer = far * 2 + (1 - core)
    routes = ((0, partner), (1, across))
    sources = (partner, across, diagonal_peer)

    def aligned(index, size):
        return pl.ds(pl.multiple_of(index * size, size), size)

    def send(src, dst, send_sem, recv_sem, **where):
        return pltpu.make_async_remote_copy(
            src_ref=src,
            dst_ref=dst,
            send_sem=send_sem,
            recv_sem=recv_sem,
            device_id=where,
            device_id_type=MESH,
        )

    pieces = [(k, 0, half) for k in range(parts - 1)]
    pieces += [(parts - 1, begin, step_k) for begin in range(0, half, step_k)]

    barrier = pltpu.get_barrier_semaphore()
    for peer in peers:
        pl.semaphore_signal(barrier, inc=1, device_id={"inner": peer}, device_id_type=MESH)
    odd, level = lax.rem(place, 2), lax.div(place, 2)
    top = lax.div(level, ring // 2 - 1)
    later = place + (1 - odd) * (2 - top) - 2 * odd
    earlier = place + odd * (2 - 3 * top) - 2 * (1 - odd)

    @pl.when(place != 1)
    def _():
        pl.semaphore_signal(barrier, inc=1, device_id={"elem": later}, device_id_type=MESH)

    @pl.when(place != 0)
    def _():
        pl.semaphore_signal(barrier, inc=1, device_id={"elem": earlier}, device_id_type=MESH)


    nodal_copy = pltpu.make_async_copy(basis.at[:, 0:2], nodal, local_sem.at[0, 0])
    nodal_copy.start()
    moved_in = [
        pltpu.make_async_copy(source, target, input_sem.at[index])
        for index, (source, target) in enumerate(
            (
                (potential_in, potential),
                (face_index_in, face_index),
                (face_match_in, face_match),
                (vectors_in, vectors),
            )
        )
    ]
    for copy in moved_in:
        copy.start()
    local = {}
    for e in range(elements):
        for k in range(parts):
            local[e, k] = pltpu.make_async_copy(
                basis.at[e, k, :, aligned(core, half)],
                own.at[e, k, aligned(core, rows)],
                local_sem.at[1 + e, k],
            )
            local[e, k].start()

    pl.semaphore_wait(barrier, inner + lax.div(place + ring - 2, ring))

    sends = []

    def launch(copy):
        copy.start()
        sends.append(copy)

    def cross_copy(piece, other):
        k, begin, size = pieces[piece]
        side = lax.rem(core + other, 2)
        return send(
            basis.at[far, k, :, pl.ds(pl.multiple_of(side * half + begin, step_k), size)],
            cross.at[k, aligned(core, rows), begin : begin + size],
            cross_send.at[other, piece],
            cross_recv.at[other, piece],
            inner=far * 2 + side,
        )

    def cross_wait(piece):
        k, begin, size = pieces[piece]
        for other in range(2):
            side = lax.rem(core + other, 2)
            send(
                basis.at[far, k, :, pl.ds(pl.multiple_of(core * half + begin, step_k), size)],
                cross.at[k, aligned(side, rows), begin : begin + size],
                cross_send.at[other, piece],
                cross_recv.at[other, piece],
                inner=far * 2 + side,
            ).wait_recv()

    def start_cross(wanted):
        for piece, (k, _, _) in enumerate(pieces):
            if k == wanted:
                for other in range(2):
                    launch(cross_copy(piece, other))

    start_cross(0)
    for e in range(elements):
        for k in range(parts):
            launch(
                send(
                    basis.at[e, k, :, aligned(1 - core, half)],
                    own.at[e, k, aligned(core, rows)],
                    pair_send.at[e, k],
                    pair_recv.at[e, k],
                    inner=partner,
                )
            )

    low, high = pl.ds(0, 2 * faced), pl.ds(2 * faced, 2 * faced)
    turn_side = lax.rem(place, 2)

    def halo(k, h, side):
        return send(
            edges.at[k, h, side],
            links.at[
                k,
                (elements - 1) * (1 - side),
                aligned(side, 2 * faced),
                h * columns : (h + 1) * columns,
            ],
            halo_send.at[k, h, side],
            halo_recv.at[k, h, side],
            elem=lax.rem(place + ring + 2 * side - 1, ring),
        )

    for copy in moved_in:
        copy.wait()
    nodal_copy.wait()

    def points_of(e):
        square = (faced, faced)
        down = lax.broadcasted_iota(jnp.int32, square, 0)
        along = lax.broadcasted_iota(jnp.int32, square, 1)
        left_row = jnp.broadcast_to(face_index[e, 0:1, :], square)
        left_column = jnp.sum(jnp.where(down == along, left_row, 0), axis=1, keepdims=True)
        matched = jnp.broadcast_to(face_match[pl.ds(e, 1), :], square) == down
        left_points = jnp.sum(
            jnp.where(matched, jnp.broadcast_to(left_column, square), 0), axis=0, keepdims=True
        )
        return jnp.concatenate([face_index[e, 1:2, :], left_points], axis=1)

    def chosen_at(points, offset):
        spots = lax.broadcasted_iota(jnp.int32, (step_k, 2 * faced), 0) + offset
        chosen = (spots == jnp.broadcast_to(points, spots.shape)).astype(jnp.float32)
        return chosen.astype(jnp.bfloat16)

    def write_faces(e, where, value, slope):
        right_value, left_value = value[:, :faced], value[:, faced:]
        right_slope, left_slope = slope[:, :faced], slope[:, faced:]
        sides = (
            0.5 * right_value - 0.25 * right_slope,
            right_value,
            -0.5 * left_value - 0.25 * left_slope,
            -left_value,
        )
        for index, side in enumerate(sides):
            faces[e, where, index * faced : (index + 1) * faced] = side.astype(jnp.bfloat16)

    for e in range(elements):
        points = points_of(e)

        def pick(index, values, e=e, points=points):
            offset = pl.multiple_of(index * step_k, step_k)
            chosen = chosen_at(points, offset)
            return tuple(
                values[k]
                + jnp.dot(
                    nodal[e, k, :, pl.ds(offset, step_k)],
                    chosen,
                    preferred_element_type=jnp.float32,
                )
                for k in range(2)
            )

        start = jnp.zeros((rows, 2 * faced), jnp.float32)
        value, slope = lax.fori_loop(0, grid // step_k, pick, (start, start))
        write_faces(e, aligned(me, rows), value, slope)

    def face_copy(d, slot, e, owner, target):
        block = faces.at[e, aligned(owner, rows)]
        return send(block, block, face_send.at[d, slot], face_recv.at[d, slot], inner=target)

    for e in range(elements):
        launch(face_copy(0, e, e, me, partner))
    launch(face_copy(1, 0, chip, me, across))
    for k in range(1, parts - 1):
        start_cross(k)

    def product(left, right):
        return lax.dot_general(
            left, right, (((1,), (1,)), ((), ())), preferred_element_type=jnp.float32
        )

    def swapped(side):
        cut = [side[:, k * faced : (k + 1) * faced] for k in range(side.shape[1] // faced)]
        order = [k + 1 - 2 * (k % 2) for k in range(len(cut))]
        return jnp.concatenate([cut[k] for k in order], axis=1)

    def weighted(row_left, row_right, left, right, k, target, scale_left, begin=0, size=half):
        @pl.loop(0, size // step_k)
        def _(index):
            offset = pl.multiple_of(begin + index * step_k, step_k)
            span = pl.ds(offset, step_k)
            there = pl.ds(pl.multiple_of(core * half + offset, step_k), step_k)
            one = left[:, span]
            if k == 0 and scale_left:
                root = jnp.sqrt(potential[row_left, there])
                one = (one.astype(jnp.float32) * root).astype(jnp.bfloat16)
                left[:, span] = one
            two = one if right is left else right[:, span]
            if k == 0 and right is not left:
                root = jnp.sqrt(potential[row_right, there])
                two = (two.astype(jnp.float32) * root).astype(jnp.bfloat16)
            term = product(one, two)
            target[...] += term if k == 0 else 0.5 * term

    for e in range(elements):
        own_sum[e] = jnp.zeros(own_sum.shape[1:], jnp.float32)
        for k in range(parts):
            local[e, k].wait()
            send(
                basis.at[e, k, :, aligned(core, half)],
                own.at[e, k, aligned(1 - core, rows)],
                pair_send.at[e, k],
                pair_recv.at[e, k],
                inner=partner,
            ).wait_recv()
            block = own.at[e, k]
            weighted(pl.ds(e, 1), pl.ds(e, 1), block, block, k, own_sum.at[e], True)
        launch(
            send(
                own_sum.at[e, aligned(1 - core, rows)],
                own_other.at[e],
                sum_send.at[e],
                sum_recv.at[e],
                inner=partner,
            )
        )

    for e in range(elements):
        face_copy(0, e, e, partner, partner).wait_recv()

    def diagonal(e, to_chip):
        return product(
            faces[e, aligned(me, rows)], swapped(faces[e, aligned(to_chip, 2 * rows)])
        ) / (4.0 * faced)

    def block_of(e, owner, to_chip):
        return operator.at[e, aligned(owner, rows), aligned(to_chip, 2 * rows)]

    def block_copy(d, slot, owner, target):
        owner_chip = owner // 2
        e = slot if slot < elements else owner_chip
        block = block_of(e, owner, owner_chip if slot < elements else 1 - owner_chip)
        return send(
            block, block, block_send.at[d, slot], block_recv.at[d, slot], inner=target
        )

    for e in range(elements):
        send(
            own_sum.at[e, aligned(core, rows)],
            own_other.at[e],
            sum_send.at[e],
            sum_recv.at[e],
            inner=partner,
        ).wait_recv()
        gram = (own_sum[e, aligned(core, rows)] + own_other[e]) / grid
        block_of(e, me, chip)[...] = (gram + diagonal(e, chip)).astype(jnp.bfloat16)
        for d, peer in routes:
            launch(block_copy(d, e, me, peer))
    start_cross(parts - 1)

    def pass_on(index, comes, goes, target):
        @pl.when(comes)
        def _():
            pl.semaphore_wait(token.at[index], 1)

        @pl.when(goes)
        def _():
            pl.semaphore_signal(
                token.at[index], inc=1, device_id={"elem": target}, device_id_type=MESH
            )

    pass_on(0, place != 0, place != 1, later)
    pass_on(1, place != 1, place != 0, earlier)

    for e in range(elements):
        current[e] = vectors[e].astype(jnp.float32)

    norm = chebyshev_norm(STEPS)
    tile = min(total, 256)
    wide = 2 * rows

    def applied_by(e, some, begin, length, values):
        return jnp.dot(
            operator[e, some, begin : begin + length],
            values,
            preferred_element_type=jnp.float32,
        )

    def through(k, e, some, cut, held):
        return jnp.dot(
            faces[e, some, cut], links[k, e, cut, held], preferred_element_type=jnp.float32
        )

    def update(k, e, some, held, applied):
        scale = (2.0 if k else 1.0) / HALF_WIDTH
        now = current[e, some, held]
        moved = scale * applied - (scale * CENTER) * now
        if k:
            moved = moved - previous[e, some, held]
        if k + 1 == STEPS:
            out[e, some, held] = moved * (1.0 / norm)
        else:
            previous[e, some, held] = now
            current[e, some, held] = moved
            state[e, some, held] = moved.astype(jnp.bfloat16)

    def coupled(e, cut, values):
        value = jnp.dot(turned[e, cut, :], values, preferred_element_type=jnp.float32)
        return (value * (1.0 / (4.0 * faced))).astype(jnp.bfloat16)

    def inside(k, of):
        for e in range(elements - 1):
            links[k, e, low] = coupled(e + 1, high, of[e + 1])
            links[k, e + 1, high] = coupled(e, low, of[e])

    def before(k):
        @pl.loop(0, total // tile)
        def _(index):
            some = pl.ds(pl.multiple_of(index * tile, tile), tile)
            for e in range(elements):
                value = applied_by(e, some, 0, total, state[e])
                if e:
                    value += through(k, e, some, high, slice(None))
                if e + 1 < elements:
                    value += through(k, e, some, low, slice(None))
                out[e, some] = value

    def after(k, h, side):
        e = (elements - 1) * (1 - side)
        held = slice(h * columns, (h + 1) * columns)
        halo(k, h, side).wait_recv()

        @pl.loop(0, total // tile)
        def _(index):
            some = pl.ds(pl.multiple_of(index * tile, tile), tile)
            applied = out[e, some, held]
            applied += through(k, e, some, aligned(side, 2 * faced), held)
            update(k, e, some, held, applied)

        if k + 1 < STEPS:
            edges[k + 1, h, 1 - side] = coupled(e, aligned(side, 2 * faced), state[e, :, held])
            launch(halo(k + 1, h, 1 - side))

    def edge_pair(k, side, values):
        e = (elements - 1) * side
        value = coupled(e, aligned(1 - side, 2 * faced), values)
        for h in range(2):
            edges[k, h, side] = value[:, h * columns : (h + 1) * columns]
            launch(halo(k, h, side))

    def far_faces():
        points = points_of(chip)
        found[...] = jnp.zeros(found.shape, jnp.float32)

        @pl.loop(0, half // step_k)
        def _(index):
            offset = pl.multiple_of(index * step_k, step_k)
            chosen = chosen_at(points, core * half + offset)
            for k in range(2):
                found[k] += jnp.dot(
                    cross[k, :, pl.ds(offset, step_k)],
                    chosen,
                    preferred_element_type=jnp.float32,
                )

        found_mine[...] = found[...].astype(jnp.bfloat16)
        swap = send(
            found_mine, found_other, face_send.at[1, 1], face_recv.at[1, 1], inner=partner
        )
        launch(swap)
        face_copy(1, 0, far, across, across).wait_recv()
        launch(face_copy(2, 0, far, across, partner))
        swap.wait_recv()
        value, slope = (found[k] + found_other[k].astype(jnp.float32) for k in range(2))
        write_faces(chip, aligned(far, 2 * rows), value, slope)
        face_copy(2, 0, far, diagonal_peer, partner).wait_recv()

    def first_partial():
        for e in range(elements):
            block_copy(1, e, across, across).wait_recv()
            launch(block_copy(2, e, across, partner))
        for e in range(elements):
            block_copy(0, e, partner, partner).wait_recv()
            block_copy(2, e, diagonal_peer, partner).wait_recv()
        for h in range(2):
            for side in range(2):
                halo(0, h, side).wait_recv()
        for e in range(elements):
            for q in range(2):
                some = slice(q * wide, (q + 1) * wide)
                value = applied_by(e, some, q * wide, wide, vectors[e, some])
                out[e, some] = value + through(0, e, some, slice(0, 4 * faced), slice(None))

    cross_sum[...] = jnp.zeros(cross_sum.shape, jnp.float32)
    for piece, (k, begin, size) in enumerate(pieces):
        if k + 1 == parts and not begin:
            first_partial()
        cross_wait(piece)
        weighted(
            pl.ds(chip, 1),
            pl.ds(chip, 1),
            own.at[chip, k],
            cross.at[k],
            k,
            cross_sum,
            False,
            begin,
            size,
        )
        if k == 1:
            far_faces()
            for e in range(elements):
                for index in range(4):
                    cut = faces[e, :, index * faced : (index + 1) * faced]
                    turn = index + 1 - 2 * (index % 2)
                    turned[e, turn * faced : (turn + 1) * faced, :] = cut.T
            for side in range(2):
                edge_pair(0, side, vectors[(elements - 1) * side])
            inside(0, vectors)
            cross_face[...] = diagonal(chip, far)
    final = send(
        cross_sum.at[aligned(1 - core, rows)],
        cross_other,
        sum_send.at[elements],
        sum_recv.at[elements],
        inner=partner,
    )
    launch(final)
    final.wait_recv()
    gram = (cross_sum[aligned(core, rows)] + cross_other[...]) / grid
    block_of(chip, me, far)[...] = (gram + cross_face[...]).astype(jnp.bfloat16)
    for d in (1, 2, 0):
        launch(block_copy(d, elements, me, sources[d]))

    def finish(e):
        mine, theirs = aligned(e, wide), aligned(1 - e, wide)
        operator[e, theirs, mine] = operator[e, mine, theirs].T
        for q in range(2):
            some = slice(q * wide, (q + 1) * wide)
            rest = slice((1 - q) * wide, (2 - q) * wide)
            applied = out[e, some]
            applied += applied_by(e, some, (1 - q) * wide, wide, vectors[e, rest])
            update(0, e, some, slice(None), applied)
        edge_pair(1, e, state[e])

    block_copy(0, elements, partner, partner).wait_recv()
    finish(chip)
    for d in (1, 2):
        block_copy(d, elements, sources[d], sources[d]).wait_recv()
    finish(far)

    for k in range(1, STEPS):
        inside(k, state)
        before(k)
        for h in range(2):
            for side in (1 - turn_side, turn_side):
                after(k, h, side)

    for copy in sends:
        copy.wait_send()


def fused(inner, ring, basis, potential, face_index, face_match, vectors):
    elements, parts, rows, grid = basis.shape
    total, width = vectors.shape[1], vectors.shape[2]
    faced = face_index.shape[2]
    half = grid // 2
    pieces = parts - 1 + half // min(half, 512)
    bf16, f32, dma = jnp.bfloat16, jnp.float32, pltpu.SemaphoreType.DMA
    vmem = pl.BlockSpec(memory_space=pltpu.VMEM)
    return pl.pallas_call(
        functools.partial(assemble_and_filter, inner, ring),
        out_shape=pltpu.VMEM(vectors.shape, f32),
        in_specs=[pl.BlockSpec(memory_space=pltpu.HBM)] * 5,
        out_specs=vmem,
        scratch_shapes=[
            pltpu.VMEM(potential.shape, f32),
            pltpu.VMEM(face_index.shape, jnp.int32),
            pltpu.VMEM(face_match.shape, jnp.int32),
            pltpu.VMEM(vectors.shape, bf16),
            pltpu.VMEM((2, 2 * rows, 2 * faced), f32),
            pltpu.VMEM((2, 2 * rows, 2 * faced), bf16),
            pltpu.VMEM((2, 2 * rows, 2 * faced), bf16),
            pltpu.VMEM((elements, parts, 2 * rows, half), bf16),
            pltpu.VMEM((parts, 2 * rows, half), bf16),
            pltpu.VMEM((elements, 2, rows, grid), bf16),
            pltpu.VMEM((elements, total, 4 * faced), bf16),
            pltpu.VMEM((elements, 4 * faced, total), bf16),
            pltpu.VMEM((elements, total, total), bf16),
            pltpu.VMEM((elements, 2 * rows, 2 * rows), f32),
            pltpu.VMEM((2 * rows, 2 * rows), f32),
            pltpu.VMEM((rows, 2 * rows), f32),
            pltpu.VMEM((elements, rows, 2 * rows), f32),
            pltpu.VMEM((rows, 2 * rows), f32),
            pltpu.VMEM((elements, total, width), bf16),
            pltpu.VMEM((STEPS, elements, 4 * faced, width), bf16),
            pltpu.VMEM((STEPS, 2, 2, 2 * faced, width // 2), bf16),
            pltpu.VMEM((elements, total, width), f32),
            pltpu.VMEM((elements, total, width), f32),
            dma((4,)),
            dma((1 + elements, parts)),
            dma((elements, parts)),
            dma((elements, parts)),
            dma((2, pieces)),
            dma((2, pieces)),
            dma((inner - 1, elements)),
            dma((inner - 1, elements)),
            dma((elements + 1,)),
            dma((elements + 1,)),
            dma((inner - 1, elements + 1)),
            dma((inner - 1, elements + 1)),
            dma((STEPS, 2, 2)),
            dma((STEPS, 2, 2)),
            pltpu.SemaphoreType.REGULAR((2,)),
        ],
        compiler_params=pltpu.CompilerParams(
            collective_id=0, has_side_effects=True, vmem_limit_bytes=60 * 1024 * 1024
        ),
    )(basis, potential, face_index, face_match, vectors)


def solution(mesh):
    inner, ring = mesh.shape["inner"], mesh.shape["elem"]
    placed = (
        P("elem", None, "inner", None),
        P("elem", None),
        P("elem", None, None),
        P("elem", None),
        P("elem", None, "inner"),
    )

    def local(basis, *rest):
        if inner == 4 and basis.shape[0] == 2 and ring >= 4 and ring % 2 == 0:
            return fused(inner, ring, basis, *rest)
        return per_device(basis, *rest)

    return jax.shard_map(
        local, mesh=mesh, in_specs=placed, out_specs=P("elem", None, "inner"), check_vma=False
    )
```
